128 devices in a mesh: row: 8 (over y, core), col: 16 (over x, z).
Axes of the slice: x: 4, y: 4, z: 4, core: 2. Of those that a mesh axis runs over, the one named last changes fastest.
Arguments:
- leaf_rhs: bfloat16 [8, 128, 2048], P('row', 'col'), may hold values from -6 to 6
- leaf_inverse: bfloat16 [8, 2048, 2048], P('row'), may hold values from -0.125 to 0.125
- interpolation: bfloat16 [8, 128, 2048], P('row'), may hold values from -0.5 to 0.5
- ranks: int32 [8], P('row'), may hold values from 32 to 128, as said below
- skeleton_rows: int32 [8, 128], P('row'), may hold values from 0 to 2047, as said below
- root_rows: int32 [8, 128], replicated, may hold values from 0 to 16383, as said below
- root_rhs: float32 [128, 16384], P('col', 'row'), may hold values from -6 to 6
- root_factor: bfloat16 [16384, 8, 2048], P('row', None, 'col')
Outputs:
- leaf_solution: float32 [8, 128, 2048], P('row', 'col')
- root_solution: float32 [128, 16384], P('col', 'row')
The draws below stay inside these ranges and needn't reach their ends.
Inputs may be any that keep to these rules, and one draw needn't show every extreme that they name: `ranks`: some leaf has rank 128. `skeleton_rows`: distinct within each leaf. `root_rows`: all distinct over all leaves and slots.
All inputs are finite; a program needn't handle non-finite values.
Results may differ from the reference program's by a relative error of at most 0.014.
Values may be sent and summed in bfloat16 or wider, within the bound.
No kernel may reach another device: no remote copies, remote signals or barrier semaphores. Data moves between devices by JAX's collectives and lax.ppermute only.
A program may use at most 128 MiB of HBM per device.

```python
import math
import jax
import jax.numpy as jnp
from jax import lax

LEAF = 2048
KMAX = 128
RT = 16384
LEAVES = 8
NRHS = 128
SECTIONS = 8
SECTION = 2048
N_ROW = 8


def draw_ranks(key, part):
    drawn = jax.random.randint(key, (LEAVES,), KMAX // 4, KMAX + 1)
    fullest = jax.random.randint(jax.random.fold_in(key, 7), (), 0, LEAVES)
    return drawn.at[fullest].set(KMAX).astype(jnp.int32)


def draw_skeleton_rows(key, part):
    leaf_keys = jax.random.split(key, LEAVES)
    chosen = jax.vmap(lambda one_key: jax.random.permutation(one_key, LEAF)[:KMAX])(leaf_keys)
    return chosen.astype(jnp.int32)


def draw_root_rows(key, part):
    order = jax.random.permutation(key, RT)[:LEAVES * KMAX]
    return order.reshape(LEAVES, KMAX).astype(jnp.int32)


def draw_root_factor(key, part):
    shape = (RT, SECTIONS, SECTION)
    noise = jax.random.normal(key, shape, jnp.float32)
    row_ids = lax.broadcasted_iota(jnp.int32, (RT, 1, 1), 0)
    block_ids = lax.broadcasted_iota(jnp.int32, (1, SECTIONS, 1), 1)
    column_ids = lax.broadcasted_iota(jnp.int32, (1, 1, SECTION), 2)
    block_gap = jnp.abs(block_ids - row_ids // SECTION)
    near_scale = 0.7 / math.sqrt(SECTION)
    far_scale = 1.0 / math.sqrt(RT)
    noise = noise * jnp.where(block_gap == 1, near_scale, far_scale)
    on_diagonal = (block_gap == 0) & (column_ids == row_ids % SECTION)
    return jnp.where(on_diagonal, noise + 1.0, noise).astype(jnp.bfloat16)


def levels(key, dims, cuts, least, top_value):
    level, own = 1.0, jax.random.fold_in(key, 6)
    for dim, parts in cuts:
        steps = jnp.exp(jax.random.uniform(jax.random.fold_in(own, dim), (parts,), jnp.float32, least / len(cuts), top_value / len(cuts)))
        level = level * jnp.repeat(steps, dims[dim] // parts).reshape([-1 if axis == dim else 1 for axis in range(len(dims))])
    return level


def centred(key, dims, scale, reach, cuts=(), kind=jnp.bfloat16):
    array = scale * jax.random.normal(key, dims, jnp.float32)
    if cuts:
        array = array * levels(key, dims, cuts, -0.22, 0.18)
    return jnp.clip(array, -reach, reach).astype(kind)


def setup_inputs(seed: int = 0) -> dict:
    splits = jax.random.split(jax.random.key(seed), 9)
    leaf_rhs = centred(splits[0], (LEAVES, NRHS, LEAF), 1.0, 6.0, ((0, 8), (1, 16)))
    leaf_inverse = centred(splits[1], (LEAVES, LEAF, LEAF), LEAF ** -0.5, 0.125, ((0, 8),))
    interpolation = centred(splits[2], (LEAVES, KMAX, LEAF), KMAX ** -0.5, 0.5, ((0, 8),))
    ranks = draw_ranks(jax.random.fold_in(splits[8], 71), 0)
    skeleton_rows = draw_skeleton_rows(jax.random.fold_in(splits[8], 71), 0)
    root_rows = draw_root_rows(jax.random.fold_in(splits[8], 71), 0)
    root_rhs = centred(splits[6], (NRHS, RT), 1.0, 6.0, ((0, 16), (1, 8)), jnp.float32)
    root_factor = draw_root_factor(jax.random.fold_in(splits[8], 71), 0)
    return {"leaf_rhs": leaf_rhs, "leaf_inverse": leaf_inverse, "interpolation": interpolation, "ranks": ranks, "skeleton_rows": skeleton_rows, "root_rows": root_rows, "root_rhs": root_rhs, "root_factor": root_factor}


def reference(leaf_rhs, leaf_inverse, interpolation, ranks, skeleton_rows, root_rows, root_rhs, root_factor):
    solved = jnp.einsum("lrk,ljk->lrj", leaf_rhs.astype(jnp.float32), leaf_inverse.astype(jnp.float32))
    live_slots = jnp.arange(KMAX, dtype=jnp.int32)[None, :] < ranks[:, None]
    index_table = jnp.broadcast_to(skeleton_rows[:, None, :], (LEAVES, NRHS, KMAX))
    skeleton = jnp.where(live_slots[:, None, :], jnp.take_along_axis(solved, index_table, axis=2), 0.0)
    flat_values = jnp.transpose(skeleton, (1, 0, 2)).reshape(NRHS, LEAVES * KMAX)
    assembled = root_rhs.at[:, root_rows.reshape(-1)].add(flat_values)
    forward_full = []
    forward_low = []
    for block_row in range(N_ROW):
        running = assembled[:, block_row * SECTION:(block_row + 1) * SECTION]
        for block_col in range(block_row):
            factor_block = root_factor[block_row * SECTION:(block_row + 1) * SECTION, block_col, :]
            running = running - jnp.dot(forward_low[block_col], factor_block.T, preferred_element_type=jnp.float32)
        forward_full.append(running)
        forward_low.append(running.astype(jnp.bfloat16))
    solution_full = [None] * N_ROW
    solution_low = [None] * N_ROW
    for block_row in reversed(range(N_ROW)):
        running = forward_full[block_row]
        for block_col in range(block_row + 1, N_ROW):
            factor_block = root_factor[block_row * SECTION:(block_row + 1) * SECTION, block_col, :]
            running = running - jnp.dot(solution_low[block_col], factor_block.T, preferred_element_type=jnp.float32)
        diagonal_block = root_factor[block_row * SECTION:(block_row + 1) * SECTION, block_row, :]
        fresh_block = jnp.dot(running.astype(jnp.bfloat16), diagonal_block.T, preferred_element_type=jnp.float32)
        solution_full[block_row] = fresh_block
        solution_low[block_row] = fresh_block.astype(jnp.bfloat16)
    root_solution = jnp.concatenate(solution_full, axis=1)
    taken = jnp.transpose(root_solution[:, root_rows], (1, 0, 2)).astype(jnp.bfloat16)
    skeleton_solution = jnp.where(live_slots[:, None, :], taken, jnp.zeros_like(taken))
    correction = jnp.einsum("lrk,lkj->lrj", skeleton_solution.astype(jnp.float32), interpolation.astype(jnp.float32))
    leaf_solution = solved - correction
    return (leaf_solution, root_solution)
```

```python
import jax
import jax.numpy as jnp
from jax import lax
from jax.sharding import PartitionSpec as P

BF = jnp.bfloat16
F32 = jnp.float32


def dot_nt(a, b):
    return lax.dot_general(a, b, (((1,), (1,)), ((), ())), preferred_element_type=F32)


def dot_nn(a, b):
    return lax.dot_general(a, b, (((1,), (0,)), ((), ())), preferred_element_type=F32)


def exchange(x, axis):
    return lax.all_to_all(x, axis, 0, 0, tiled=True)


def split_columns(x, parts):
    rows, width = x.shape
    return jnp.transpose(x.reshape(rows, parts, width // parts), (1, 0, 2))


def on_device(
    leaf_rhs, leaf_inverse, interpolation, ranks, skeleton_rows, root_rows, root_rhs, root_factor
):
    row_at = lax.axis_index("row")
    n_row = lax.axis_size("row")
    n_col = lax.axis_size("col")
    rhs_here = leaf_rhs.shape[1]
    n_rhs = rhs_here * n_col
    slots = skeleton_rows.shape[1]
    section = root_rhs.shape[1]
    width = section // n_col
    leaf = leaf_rhs.shape[2]

    run = exchange(split_columns(root_rhs, n_col), "col").reshape(n_rhs, width)

    factor = root_factor.reshape(section, n_row * width)
    diagonal = lax.dynamic_slice_in_dim(factor, row_at * width, width, 1)
    diagonal_full = lax.all_gather(diagonal, "col", axis=1, tiled=True)
    folded = dot_nn(diagonal_full, factor).astype(BF)

    solved = dot_nt(leaf_rhs[0], leaf_inverse[0])
    live = jnp.arange(slots, dtype=jnp.int32) < ranks[0]
    chosen = jnp.where(live, skeleton_rows[0], -1)
    pick = (jnp.arange(leaf, dtype=jnp.int32)[:, None] == chosen[None, :]).astype(BF)
    skeleton = dot_nn(solved.astype(BF), pick).astype(BF)
    everyone = jnp.broadcast_to(skeleton[None], (n_row * n_col, rhs_here, slots))
    gathered = exchange(everyone, ("row", "col")).reshape(n_row, n_rhs, slots)
    gathered = jnp.transpose(gathered, (1, 0, 2)).reshape(n_rhs, n_row * slots)
    first = row_at * section + lax.axis_index("col") * width
    own_rows = first + jnp.arange(width, dtype=jnp.int32)
    place = (root_rows.reshape(-1)[:, None] == own_rows[None, :]).astype(BF)
    run = run + dot_nn(gathered, place)

    def reduce_columns(partial):
        tiles = exchange(split_columns(partial.astype(BF), n_col), "col")
        return jnp.sum(tiles.astype(F32), axis=0)

    last = n_row - 1
    low = run.astype(BF)
    known = low
    for j in range(last - 1):
        arrived = lax.ppermute(known, "row", [(j, j + 1)])
        run = run - reduce_columns(dot_nt(arrived, factor[:, : (j + 1) * width]))
        low = run.astype(BF)
        known = jnp.concatenate([arrived, low], axis=1)
    arrived = lax.ppermute(known, "row", [(last - 1, last)])
    own = dot_nt(low, diagonal)
    back = reduce_columns(own - dot_nt(arrived, folded[:, : last * width]))
    known = back.astype(BF)
    for i in reversed(range(1, last)):
        arrived = lax.ppermute(known, "row", [(i + 1, i)])
        fresh = reduce_columns(own - dot_nt(arrived, folded[:, (i + 1) * width :]))
        back = jnp.where(row_at == i, fresh, back)
        known = jnp.concatenate([fresh.astype(BF), arrived], axis=1)
    arrived = lax.ppermute(known, "row", [(1, 0)])
    partial = (own - dot_nt(arrived, folded[:, width:])).astype(BF)
    done = back.astype(BF).reshape(n_col, rhs_here, width)
    mixed = jnp.concatenate([partial.reshape(n_col, rhs_here, section), done], axis=2)
    mixed = exchange(mixed, "col")
    summed = jnp.sum(mixed[:, :, :section].astype(F32), axis=0)
    placed = jnp.transpose(mixed[:, :, section:], (1, 0, 2)).reshape(rhs_here, section)
    root_solution = jnp.where(row_at == 0, summed, placed.astype(F32))

    block_rows = row_at * section + jnp.arange(section, dtype=jnp.int32)
    take = (block_rows[:, None] == root_rows.reshape(-1)[None, :]).astype(BF)
    taken = dot_nn(root_solution.astype(BF), take).astype(BF)
    taken = exchange(split_columns(taken, n_row), "row")
    taken = jnp.sum(taken.astype(F32), axis=0)
    taken = jnp.where(live[None, :], taken, 0.0).astype(BF)
    leaf_solution = solved - dot_nn(taken, interpolation[0])
    return (leaf_solution[None], root_solution)


def solution(mesh):
    in_specs = (
        P("row", "col", None),
        P("row", None, None),
        P("row", None, None),
        P("row"),
        P("row", None),
        P(),
        P("col", "row"),
        P("row", None, "col"),
    )
    out_specs = (P("row", "col", None), P("col", "row"))
    return jax.shard_map(
        on_device, mesh=mesh, in_specs=in_specs, out_specs=out_specs, check_vma=False
    )
```

```python
import jax
import jax.numpy as jnp
from jax import lax
from jax.sharding import PartitionSpec as P

BF = jnp.bfloat16
F32 = jnp.float32


def dot_nt(a, b):
    return lax.dot_general(a, b, (((1,), (1,)), ((), ())), preferred_element_type=F32)


def dot_nn(a, b):
    return lax.dot_general(a, b, (((1,), (0,)), ((), ())), preferred_element_type=F32)


def exchange(x, axis):
    return lax.all_to_all(x, axis, 0, 0, tiled=True)


def split_columns(x, parts):
    rows, width = x.shape
    return jnp.transpose(x.reshape(rows, parts, width // parts), (1, 0, 2))


def on_device(
    leaf_rhs, leaf_inverse, interpolation, ranks, skeleton_rows, root_rows, root_rhs, root_factor
):
    row_at = lax.axis_index("row")
    n_row = lax.axis_size("row")
    n_col = lax.axis_size("col")
    rhs_here = leaf_rhs.shape[1]
    n_rhs = rhs_here * n_col
    slots = skeleton_rows.shape[1]
    section = root_rhs.shape[1]
    width = section // n_col
    leaf = leaf_rhs.shape[2]

    run = exchange(split_columns(root_rhs, n_col), "col").reshape(n_rhs, width)

    solved = dot_nt(leaf_rhs[0], leaf_inverse[0])
    live = jnp.arange(slots, dtype=jnp.int32) < ranks[0]
    chosen = jnp.where(live, skeleton_rows[0], -1)
    pick = (jnp.arange(leaf, dtype=jnp.int32)[:, None] == chosen[None, :]).astype(BF)
    skeleton = dot_nn(solved.astype(BF), pick).astype(BF)

    root_factor, skeleton = lax.optimization_barrier((root_factor, skeleton))
    factor = root_factor.reshape(section, n_row * width)
    diagonal = lax.dynamic_slice_in_dim(factor, row_at * width, width, 1)
    diagonal_full = lax.all_gather(diagonal, "col", axis=1, tiled=True)
    folded = dot_nn(diagonal_full, factor).astype(BF)

    everyone = jnp.broadcast_to(skeleton[None], (n_row * n_col, rhs_here, slots))
    gathered = exchange(everyone, ("row", "col")).reshape(n_row, n_rhs, slots)
    gathered = jnp.transpose(gathered, (1, 0, 2)).reshape(n_rhs, n_row * slots)
    first = row_at * section + lax.axis_index("col") * width
    own_rows = first + jnp.arange(width, dtype=jnp.int32)
    place = (root_rows.reshape(-1)[:, None] == own_rows[None, :]).astype(BF)
    run = run + dot_nn(gathered, place)

    def reduce_columns(partial):
        tiles = exchange(split_columns(partial.astype(BF), n_col), "col")
        return jnp.sum(tiles.astype(F32), axis=0)

    def on_turn(turn, step, old, *operands):
        return lax.cond(row_at == turn, step, lambda old, *rest: old, old, *operands)

    last = n_row - 1
    known = run.astype(BF)
    for j in range(last - 1):
        arrived = lax.ppermute(known, "row", [(j, j + 1)])

        def forward(run, arrived, factor, j=j):
            return run - reduce_columns(dot_nt(arrived, factor[:, : (j + 1) * width]))

        run = on_turn(j + 1, forward, run, arrived, factor)
        known = jnp.concatenate([arrived, run.astype(BF)], axis=1)
    arrived = lax.ppermute(known, "row", [(last - 1, last)])

    def turn_round(run, arrived, diagonal, folded):
        return reduce_columns(
            dot_nt(run.astype(BF), diagonal) - dot_nt(arrived, folded[:, : last * width])
        )

    run = on_turn(last, turn_round, run, arrived, diagonal, folded)
    known = run.astype(BF)
    for i in reversed(range(1, last)):
        arrived = lax.ppermute(known, "row", [(i + 1, i)])

        def backward(run, arrived, diagonal, folded, i=i):
            return reduce_columns(
                dot_nt(run.astype(BF), diagonal) - dot_nt(arrived, folded[:, (i + 1) * width :])
            )

        run = on_turn(i, backward, run, arrived, diagonal, folded)
        known = jnp.concatenate([run.astype(BF), arrived], axis=1)
    arrived = lax.ppermute(known, "row", [(1, 0)])

    def gather_rhs(run, arrived, diagonal, folded):
        done = exchange(run.astype(BF).reshape(n_col, rhs_here, width), "col")
        return jnp.transpose(done, (1, 0, 2)).reshape(rhs_here, section).astype(F32)

    def finish(run, arrived, diagonal, folded):
        partial = dot_nt(run.astype(BF), diagonal) - dot_nt(arrived, folded[:, width:])
        tiles = exchange(partial.astype(BF).reshape(n_col, rhs_here, section), "col")
        return jnp.sum(tiles.astype(F32), axis=0)

    root_solution = lax.cond(row_at == 0, finish, gather_rhs, run, arrived, diagonal, folded)

    block_rows = row_at * section + jnp.arange(section, dtype=jnp.int32)
    take = (block_rows[:, None] == root_rows.reshape(-1)[None, :]).astype(BF)
    taken = dot_nn(root_solution.astype(BF), take).astype(BF)
    taken = exchange(split_columns(taken, n_row), "row")
    taken = jnp.sum(taken.astype(F32), axis=0)
    taken = jnp.where(live[None, :], taken, 0.0).astype(BF)
    leaf_solution = solved - dot_nn(taken, interpolation[0])
    return (leaf_solution[None], root_solution)


def solution(mesh):
    in_specs = (
        P("row", "col", None),
        P("row", None, None),
        P("row", None, None),
        P("row"),
        P("row", None),
        P(),
        P("col", "row"),
        P("row", None, "col"),
    )
    out_specs = (P("row", "col", None), P("col", "row"))
    return jax.shard_map(
        on_device, mesh=mesh, in_specs=in_specs, out_specs=out_specs, check_vma=False
    )
```

```python
import jax
import jax.numpy as jnp
from jax import lax
from jax.sharding import PartitionSpec as P

BF = jnp.bfloat16
F32 = jnp.float32


def dot_nt(a, b):
    return lax.dot_general(a, b, (((1,), (1,)), ((), ())), preferred_element_type=F32)


def dot_nn(a, b):
    return lax.dot_general(a, b, (((1,), (0,)), ((), ())), preferred_element_type=F32)


def exchange(x, axis):
    return lax.all_to_all(x, axis, 0, 0, tiled=True)


def split_columns(x, parts):
    rows, width = x.shape
    return jnp.transpose(x.reshape(rows, parts, width // parts), (1, 0, 2))


def on_device(
    leaf_rhs, leaf_inverse, interpolation, ranks, skeleton_rows, root_rows, root_rhs, root_factor
):
    row_at = lax.axis_index("row")
    n_row = lax.axis_size("row")
    n_col = lax.axis_size("col")
    rhs_here = leaf_rhs.shape[1]
    n_rhs = rhs_here * n_col
    slots = skeleton_rows.shape[1]
    section = root_rhs.shape[1]
    half = section // 2
    width = section // n_col
    leaf = leaf_rhs.shape[2]
    even = row_at % 2 == 0
    up = [(r, r + 1) for r in range(0, n_row, 2)]
    down = [(r + 1, r) for r in range(0, n_row, 2)]

    run = exchange(split_columns(root_rhs, n_col), "col").reshape(n_rhs, width)

    solved = dot_nt(leaf_rhs[0], leaf_inverse[0])
    live = jnp.arange(slots, dtype=jnp.int32) < ranks[0]
    chosen = jnp.where(live, skeleton_rows[0], -1)
    pick = (jnp.arange(leaf, dtype=jnp.int32)[:, None] == chosen[None, :]).astype(BF)
    skeleton = dot_nn(solved.astype(BF), pick).astype(BF)

    diagonal = lax.dynamic_index_in_dim(root_factor, row_at, 1, keepdims=False)
    above = lax.dynamic_index_in_dim(root_factor, row_at | 1, 1, keepdims=False)
    lower = lax.ppermute(above[half:], "row", up)
    above = jnp.where(even, above[:half], lower)
    whole = lax.all_gather(
        jnp.concatenate([diagonal, above], axis=0), "col", axis=1, tiled=True
    )

    skeleton, run, root_factor = lax.optimization_barrier((skeleton, run, root_factor))
    everyone = jnp.broadcast_to(skeleton[None], (n_row * n_col, rhs_here, slots))
    gathered = exchange(everyone, ("row", "col")).reshape(n_row, n_rhs, slots)
    gathered = jnp.transpose(gathered, (1, 0, 2)).reshape(n_rhs, n_row * slots)
    first = row_at * section + lax.axis_index("col") * width
    own_rows = first + jnp.arange(width, dtype=jnp.int32)
    place = (root_rows.reshape(-1)[:, None] == own_rows[None, :]).astype(BF)
    run = run + dot_nn(gathered, place)

    factor = root_factor.reshape(section, n_row * width)

    last = n_row - 1

    def reduce_columns(partial):
        tiles = exchange(split_columns(partial.astype(BF), n_col), "col")
        return jnp.sum(tiles.astype(F32), axis=0)

    def on_turn(turn, step, old, *operands):
        return lax.cond(turn, step, lambda old, *rest: old, old, *operands)

    known = run.astype(BF)
    for j in range(last - 1):
        arrived = lax.ppermute(known, "row", [(j, j + 1)])

        def forward(run, arrived, factor, j=j):
            return run - reduce_columns(dot_nt(arrived, factor[:, : (j + 1) * width]))

        run = on_turn(row_at == j + 1, forward, run, arrived, factor)
        known = jnp.concatenate([arrived, run.astype(BF)], axis=1)
        if j == last - 4:
            held, _ = lax.optimization_barrier((factor, known))
            folded = dot_nn(whole[:section], held).astype(BF)

    def merge_pair(folded, whole, factor):
        odd_part = lax.ppermute(factor, "row", down[:-1])
        odd_part = jnp.where(even, odd_part, factor)
        through = dot_nn(whole[section:], odd_part).astype(BF)
        through = jnp.concatenate([through, lax.ppermute(through, "row", down[:-1])], axis=0)

        def merge_even(folded, whole, through):
            passed = dot_nn(whole[:section], through)
            later = jnp.arange(n_row * width, dtype=jnp.int32) // width > row_at + 1
            return jnp.where(later[None, :], folded.astype(F32) - passed, passed).astype(BF)

        return lax.cond(
            even, merge_even, lambda folded, *rest: folded, folded, whole, through
        )

    held, _ = lax.optimization_barrier((whole, known))
    own_block = jnp.arange(n_row * width, dtype=jnp.int32) // width == row_at
    merged = lax.cond(
        row_at < last - 1,
        merge_pair,
        lambda folded, *rest: jnp.zeros_like(folded),
        folded,
        held,
        jnp.where(own_block[None, :], factor, folded),
    )
    arrived = lax.ppermute(known, "row", [(last - 1, last)])
    arrived, merged = lax.optimization_barrier((arrived, merged))

    def solve_last(run, arrived, diagonal, folded):
        return reduce_columns(
            dot_nt(run.astype(BF), diagonal) - dot_nt(arrived, folded[:, : last * width])
        )

    run = on_turn(row_at == last, solve_last, run, arrived, diagonal, folded)
    low = run.astype(BF)
    arrived = lax.ppermute(low, "row", [(last, last - 1)])

    def solve_next(run, arrived, diagonal, folded):
        return reduce_columns(
            dot_nt(run.astype(BF), diagonal) - dot_nt(arrived, folded[:, last * width :])
        )

    run = on_turn(row_at == last - 1, solve_next, run, arrived, diagonal, folded)
    low = run.astype(BF)

    other = lax.ppermute(low, "row", down)
    block = lax.dynamic_slice_in_dim(merged, (row_at | 1) * width, width, 1)
    known = jnp.concatenate([low, arrived], axis=1)
    known = (
        lax.ppermute(known, "row", [(last - 1, last - 3)])
        + lax.ppermute(known, "row", [(last - 1, last - 2)])
    )

    def partial_sum(low, other, known, diagonal, block, merged, start):
        own = dot_nt(low, diagonal) - dot_nt(known, merged[:, start:])
        return own - jnp.where(even, dot_nt(other, block), 0.0)

    for pair in (2, 1):
        start = (2 * pair + 2) * width

        def backward(run, low, other, known, diagonal, block, merged, start=start):
            return reduce_columns(partial_sum(low, other, known, diagonal, block, merged, start))

        run = on_turn(
            row_at // 2 == pair, backward, run, low, other, known, diagonal, block, merged
        )
        low = run.astype(BF)
        same = [(2 * pair, 2 * pair - 2), (2 * pair + 1, 2 * pair - 1)]
        cross = [(2 * pair, 2 * pair - 1), (2 * pair + 1, 2 * pair - 2)]
        same = lax.ppermute(jnp.concatenate([low, known], axis=1), "row", same)
        cross = lax.ppermute(low, "row", cross)
        same, older = same[:, :width], same[:, width:]
        known = jnp.concatenate(
            [jnp.where(even, same, cross), jnp.where(even, cross, same), older], axis=1
        )

    def gather_rhs(low, other, known, diagonal, block, merged):
        done = exchange(low.reshape(n_col, rhs_here, width), "col")
        return jnp.transpose(done, (1, 0, 2)).reshape(rhs_here, section).astype(F32)

    def finish(low, other, known, diagonal, block, merged):
        partial = partial_sum(low, other, known, diagonal, block, merged, 2 * width)
        tiles = exchange(partial.astype(BF).reshape(n_col, rhs_here, section), "col")
        return jnp.sum(tiles.astype(F32), axis=0)

    root_solution = lax.cond(
        row_at < 2, finish, gather_rhs, low, other, known, diagonal, block, merged
    )

    block_rows = row_at * section + jnp.arange(section, dtype=jnp.int32)
    take = (block_rows[:, None] == root_rows.reshape(-1)[None, :]).astype(BF)
    taken = dot_nn(root_solution.astype(BF), take).astype(BF)
    taken = exchange(split_columns(taken, n_row), "row")
    taken = jnp.sum(taken.astype(F32), axis=0)
    taken = jnp.where(live[None, :], taken, 0.0).astype(BF)
    leaf_solution = solved - dot_nn(taken, interpolation[0])
    return (leaf_solution[None], root_solution)


def solution(mesh):
    in_specs = (
        P("row", "col", None),
        P("row", None, None),
        P("row", None, None),
        P("row"),
        P("row", None),
        P(),
        P("col", "row"),
        P("row", None, "col"),
    )
    out_specs = (P("row", "col", None), P("col", "row"))
    return jax.shard_map(
        on_device, mesh=mesh, in_specs=in_specs, out_specs=out_specs, check_vma=False
    )
```

```python
import jax
import jax.numpy as jnp
from jax import lax
from jax.experimental import pallas as pl
from jax.experimental.pallas import tpu as pltpu
from jax.sharding import PartitionSpec as P


BF = jnp.bfloat16
F32 = jnp.float32


def dot_nt(a, b):
    return lax.dot_general(a, b, (((1,), (1,)), ((), ())), preferred_element_type=F32)


def dot_nn(a, b):
    return lax.dot_general(a, b, (((1,), (0,)), ((), ())), preferred_element_type=F32)


def exchange(x, axis):
    return lax.all_to_all(x, axis, 0, 0, tiled=True)


def split_columns(x, parts):
    rows, width = x.shape
    return jnp.transpose(x.reshape(rows, parts, width // parts), (1, 0, 2))


def fold_kernel(at_ref, left_ref, right_ref, own_ref, out_ref):
    step = pl.program_id(0)
    first, own = at_ref[0], at_ref[1]

    @pl.when(step >= first)
    def _():
        total = jnp.dot(left_ref[...], right_ref[...], preferred_element_type=F32)
        width = out_ref.shape[1] // 2
        for part in range(2):
            here = slice(part * width, (part + 1) * width)
            kept = (2 * step + part == own).astype(F32)
            out_ref[:, here] = jnp.where(
                kept > 0.5, own_ref[:, here], total[:, here].astype(out_ref.dtype)
            )


def merge_kernel(at_ref, left_ref, high_ref, low_ref, folded_ref, out_ref):
    step = pl.program_id(0)
    first, own = at_ref[0], at_ref[1]

    @pl.when(step >= first)
    def _():
        half = high_ref.shape[0]
        total = jnp.dot(left_ref[:, :half], high_ref[...], preferred_element_type=F32)
        total += jnp.dot(left_ref[:, half:], low_ref[...], preferred_element_type=F32)
        width = out_ref.shape[1] // 2
        for part in range(2):
            here = slice(part * width, (part + 1) * width)
            later = (2 * step + part > own + 1).astype(F32)
            out_ref[:, here] = (
                jnp.where(later > 0.5, folded_ref[:, here].astype(F32) - total[:, here], total[:, here])
            ).astype(out_ref.dtype)


def chunked(kernel, at, left, rows, left_block, rights, out_columns, chunk):
    def column(step, at):
        return (0, jnp.maximum(step, at[0]))

    grid_spec = pltpu.PrefetchScalarGridSpec(
        num_scalar_prefetch=1,
        grid=(out_columns // chunk,),
        in_specs=[pl.BlockSpec((rows, left.shape[1]), lambda step, at: (left_block, 0))]
        + [pl.BlockSpec((x.shape[0], chunk), column) for x in rights],
        out_specs=pl.BlockSpec((rows, chunk), column),
    )
    return pl.pallas_call(
        kernel,
        grid_spec=grid_spec,
        out_shape=jax.ShapeDtypeStruct((rows, out_columns), BF),
    )(at, left, *rights)


def through_kernel(at_ref, left_ref, right_ref, out_ref):
    @pl.when(pl.program_id(0) >= at_ref[0])
    def _():
        out_ref[...] = jnp.dot(
            left_ref[...], right_ref[...], preferred_element_type=F32
        ).astype(out_ref.dtype)


def on_device(
    leaf_rhs, leaf_inverse, interpolation, ranks, skeleton_rows, root_rows, root_rhs, root_factor
):
    row_at = lax.axis_index("row")
    n_row = lax.axis_size("row")
    n_col = lax.axis_size("col")
    rhs_here = leaf_rhs.shape[1]
    n_rhs = rhs_here * n_col
    slots = skeleton_rows.shape[1]
    section = root_rhs.shape[1]
    half = section // 2
    width = section // n_col
    leaf = leaf_rhs.shape[2]
    even = row_at % 2 == 0
    up = [(r, r + 1) for r in range(0, n_row, 2)]
    down = [(r + 1, r) for r in range(0, n_row, 2)]

    solved = dot_nt(leaf_rhs[0], leaf_inverse[0])
    live = jnp.arange(slots, dtype=jnp.int32) < ranks[0]
    chosen = jnp.where(live, skeleton_rows[0], -1)
    pick = (jnp.arange(leaf, dtype=jnp.int32)[:, None] == chosen[None, :]).astype(BF)
    skeleton = dot_nn(solved.astype(BF), pick).astype(BF)

    diagonal = lax.dynamic_index_in_dim(root_factor, row_at, 1, keepdims=False)
    above = lax.dynamic_index_in_dim(root_factor, row_at | 1, 1, keepdims=False)
    lower = lax.ppermute(above[half:], "row", up)
    above = jnp.where(even, above[:half], lower)
    held = jnp.concatenate([diagonal, above], axis=0)
    whole = lax.all_gather(held, "col", axis=1, tiled=True)

    spread = exchange(jnp.broadcast_to(skeleton[None], (n_row, rhs_here, slots)), "row")
    spread = jnp.transpose(spread, (1, 0, 2)).reshape(rhs_here, n_row * slots)
    block_rows = row_at * section + jnp.arange(section, dtype=jnp.int32)
    place = (root_rows.reshape(-1)[:, None] == block_rows[None, :]).astype(BF)
    run = split_columns(root_rhs + dot_nn(spread, place), n_col)
    run = exchange(run, "col")
    run = run.reshape(n_rhs, width)

    factor = root_factor.reshape(section, n_row * width)

    last = n_row - 1

    def reduce_columns(partial):
        tiles = exchange(split_columns(partial.astype(BF), n_col), "col")
        return jnp.sum(tiles.astype(F32), axis=0)

    def on_turn(turn, step, old, *operands):
        return lax.cond(turn, step, lambda old, *rest: old, old, *operands)

    known = run.astype(BF)
    for j in range(last - 1):
        arrived = lax.ppermute(known, "row", [(j, j + 1)])

        def forward(run, arrived, factor, j=j):
            return run - reduce_columns(dot_nt(arrived, factor[:, : (j + 1) * width]))

        run = on_turn(row_at == j + 1, forward, run, arrived, factor)
        known = jnp.concatenate([arrived, run.astype(BF)], axis=1)
        if j == last - 4:
            held, _ = lax.optimization_barrier((factor, known))
            first = jnp.where(row_at == last, 0, row_at // 2)
            at = jnp.stack([first, row_at]).astype(jnp.int32)
            folded = chunked(
                fold_kernel, at, whole, section, 0, (held, held), n_row * width, 2 * width
            )

    def merge_pair(at, whole, folded):
        odd_part = lax.ppermute(folded, "row", down[:-1])

        def pass_through(odd_part, _=None):
            return chunked(
                through_kernel, at, whole, half, 2, (odd_part,), n_row * width, 2 * width
            )

        through = lax.cond(even, pass_through, lambda _, own: pass_through(own), odd_part, folded)
        low_half = lax.ppermute(through, "row", down[:-1])

        def merge_even(at, whole, through, low_half, folded):
            rights = (through, low_half, folded)
            return chunked(merge_kernel, at, whole, section, 0, rights, n_row * width, 2 * width)

        return lax.cond(
            even,
            merge_even,
            lambda at, whole, through, low_half, folded: folded,
            at,
            whole,
            through,
            low_half,
            folded,
        )

    held, _ = lax.optimization_barrier((whole, known))
    merged = lax.cond(
        row_at < last - 1,
        merge_pair,
        lambda at, whole, folded: jnp.zeros_like(folded),
        at,
        held,
        folded,
    )
    arrived = lax.ppermute(known, "row", [(last - 1, last)])
    arrived, merged = lax.optimization_barrier((arrived, merged))

    def solve_last(run, arrived, diagonal, folded):
        return reduce_columns(
            dot_nt(run.astype(BF), diagonal) - dot_nt(arrived, folded[:, : last * width])
        )

    run = on_turn(row_at == last, solve_last, run, arrived, diagonal, folded)
    low = run.astype(BF)
    arrived = lax.ppermute(low, "row", [(last, last - 1)])

    def solve_next(run, arrived, diagonal, folded):
        return reduce_columns(
            dot_nt(run.astype(BF), diagonal) - dot_nt(arrived, folded[:, last * width :])
        )

    run = on_turn(row_at == last - 1, solve_next, run, arrived, diagonal, folded)
    low = run.astype(BF)

    other = lax.ppermute(low, "row", down)
    block = lax.dynamic_slice_in_dim(merged, (row_at | 1) * width, width, 1)
    known = jnp.concatenate([low, arrived], axis=1)
    known = (
        lax.ppermute(known, "row", [(last - 1, last - 3)])
        + lax.ppermute(known, "row", [(last - 1, last - 2)])
    )

    def partial_sum(low, other, known, diagonal, block, merged, start):
        own = dot_nt(low, diagonal) - dot_nt(known, merged[:, start:])
        return own - jnp.where(even, dot_nt(other, block), 0.0)

    for pair in (2, 1):
        start = (2 * pair + 2) * width

        def backward(run, low, other, known, diagonal, block, merged, start=start):
            return reduce_columns(partial_sum(low, other, known, diagonal, block, merged, start))

        run = on_turn(
            row_at // 2 == pair, backward, run, low, other, known, diagonal, block, merged
        )
        low = run.astype(BF)
        same = [(2 * pair, 2 * pair - 2), (2 * pair + 1, 2 * pair - 1)]
        cross = [(2 * pair, 2 * pair - 1), (2 * pair + 1, 2 * pair - 2)]
        same = lax.ppermute(jnp.concatenate([low, known], axis=1), "row", same)
        cross = lax.ppermute(low, "row", cross)
        same, older = same[:, :width], same[:, width:]
        known = jnp.concatenate(
            [jnp.where(even, same, cross), jnp.where(even, cross, same), older], axis=1
        )

    def gather_rhs(low, other, known, diagonal, block, merged):
        done = exchange(low.reshape(n_col, rhs_here, width), "col")
        return jnp.transpose(done, (1, 0, 2)).reshape(rhs_here, section).astype(F32)

    def finish(low, other, known, diagonal, block, merged):
        partial = partial_sum(low, other, known, diagonal, block, merged, 2 * width)
        tiles = exchange(partial.astype(BF).reshape(n_col, rhs_here, section), "col")
        return jnp.sum(tiles.astype(F32), axis=0)

    root_solution = lax.cond(
        row_at < 2, finish, gather_rhs, low, other, known, diagonal, block, merged
    )

    take = (block_rows[:, None] == root_rows.reshape(-1)[None, :]).astype(BF)
    taken = dot_nn(root_solution.astype(BF), take).astype(BF)
    taken = exchange(split_columns(taken, n_row), "row")
    taken = jnp.sum(taken.astype(F32), axis=0)
    taken = jnp.where(live[None, :], taken, 0.0).astype(BF)
    leaf_solution = solved - dot_nn(taken, interpolation[0])
    return (leaf_solution[None], root_solution)


def solution(mesh):
    in_specs = (
        P("row", "col", None),
        P("row", None, None),
        P("row", None, None),
        P("row"),
        P("row", None),
        P(),
        P("col", "row"),
        P("row", None, "col"),
    )
    out_specs = (P("row", "col", None), P("col", "row"))

    return jax.shard_map(
        on_device, mesh=mesh, in_specs=in_specs, out_specs=out_specs, check_vma=False
    )
```

```python
import jax
import jax.numpy as jnp
from jax import lax
from jax.experimental import pallas as pl
from jax.experimental.pallas import tpu as pltpu
from jax.sharding import PartitionSpec as P


BF = jnp.bfloat16
F32 = jnp.float32


def dot_nt(a, b):
    return lax.dot_general(a, b, (((1,), (1,)), ((), ())), preferred_element_type=F32)


def dot_nn(a, b):
    return lax.dot_general(a, b, (((1,), (0,)), ((), ())), preferred_element_type=F32)


def exchange(x, axis):
    return lax.all_to_all(x, axis, 0, 0, tiled=True)


def split_columns(x, parts):
    rows, width = x.shape
    return jnp.transpose(x.reshape(rows, parts, width // parts), (1, 0, 2))


def fold_kernel(at_ref, right_ref, left_ref, out_ref):
    step = pl.program_id(0)
    first, own = at_ref[0], at_ref[1]

    @pl.when(step >= first)
    def _():
        total = jnp.dot(left_ref[...], right_ref[...], preferred_element_type=F32)
        width = out_ref.shape[0] // 2
        for part in range(2):
            here = slice(part * width, (part + 1) * width)
            kept = (2 * step + part == own).astype(F32)
            out_ref[here, :] = jnp.where(
                kept > 0.5, left_ref[here, :], total[here, :].astype(out_ref.dtype)
            )


def through_kernel(at_ref, right_ref, left_ref, out_ref):
    @pl.when(pl.program_id(0) >= at_ref[0])
    def _():
        out_ref[...] = jnp.dot(
            left_ref[...], right_ref[...], preferred_element_type=F32
        ).astype(out_ref.dtype)


def merge_kernel(at_ref, right_ref, high_ref, low_ref, folded_ref, out_ref):
    step = pl.program_id(0)
    first, own = at_ref[0], at_ref[1]

    @pl.when(step >= first)
    def _():
        half = high_ref.shape[1]
        total = jnp.dot(high_ref[...], right_ref[:half, :], preferred_element_type=F32)
        total += jnp.dot(low_ref[...], right_ref[half:, :], preferred_element_type=F32)
        width = out_ref.shape[0] // 2
        for part in range(2):
            here = slice(part * width, (part + 1) * width)
            block = 2 * step + part
            kept = (block != own + 1).astype(F32)
            passed = (block != own).astype(F32)
            old = jnp.where(kept > 0.5, folded_ref[here, :].astype(F32), 0.0)
            new = jnp.where(passed > 0.5, total[here, :], 0.0)
            new = jnp.where(kept > 0.5, -new, new)
            out_ref[here, :] = (old + new).astype(out_ref.dtype)


def chunked(kernel, at, right, columns, right_block, lefts, chunk):
    def row(step, at):
        return (jnp.maximum(step, at[0]), 0)

    rows = lefts[0].shape[0]
    grid_spec = pltpu.PrefetchScalarGridSpec(
        num_scalar_prefetch=1,
        grid=(rows // chunk,),
        in_specs=[pl.BlockSpec((right.shape[0], columns), lambda step, at: (0, right_block))]
        + [pl.BlockSpec((chunk, x.shape[1]), row) for x in lefts],
        out_specs=pl.BlockSpec((chunk, columns), row),
    )
    return pl.pallas_call(
        kernel,
        grid_spec=grid_spec,
        out_shape=jax.ShapeDtypeStruct((rows, columns), BF),
    )(at, right, *lefts)


def on_device(
    leaf_rhs, leaf_inverse, interpolation, ranks, skeleton_rows, root_rows, root_rhs, root_factor
):
    row_at = lax.axis_index("row")
    n_row = lax.axis_size("row")
    n_col = lax.axis_size("col")
    rhs_here = leaf_rhs.shape[1]
    n_rhs = rhs_here * n_col
    slots = skeleton_rows.shape[1]
    section = root_rhs.shape[1]
    half = section // 2
    width = section // n_col
    leaf = leaf_rhs.shape[2]
    even = row_at % 2 == 0
    up = [(r, r + 1) for r in range(0, n_row, 2)]
    down = [(r + 1, r) for r in range(0, n_row, 2)]

    solved = dot_nt(leaf_rhs[0], leaf_inverse[0])
    live = jnp.arange(slots, dtype=jnp.int32) < ranks[0]
    chosen = jnp.where(live, skeleton_rows[0], -1)
    pick = (jnp.arange(leaf, dtype=jnp.int32)[:, None] == chosen[None, :]).astype(BF)
    skeleton = dot_nn(solved.astype(BF), pick).astype(BF)

    factor = jnp.transpose(root_factor, (1, 2, 0)).reshape(n_row * width, section)
    diagonal = lax.dynamic_slice_in_dim(factor, row_at * width, width, 0)
    above = lax.dynamic_slice_in_dim(factor, (row_at | 1) * width, width, 0)

    lower = lax.ppermute(above[:, half:], "row", up)
    held = jnp.concatenate([diagonal, jnp.where(even, above[:, :half], lower)], axis=1)
    whole = lax.all_gather(held, "col", axis=0, tiled=True)

    spread = exchange(jnp.broadcast_to(skeleton[None], (n_row, rhs_here, slots)), "row")
    spread = jnp.transpose(spread, (1, 0, 2)).reshape(rhs_here, n_row * slots)
    block_rows = row_at * section + jnp.arange(section, dtype=jnp.int32)
    place = (root_rows.reshape(-1)[:, None] == block_rows[None, :]).astype(BF)
    run = split_columns(root_rhs + dot_nn(spread, place), n_col)
    run = exchange(run, "col")
    run = run.reshape(n_rhs, width)

    last = n_row - 1

    def reduce_columns(partial):
        tiles = exchange(split_columns(partial.astype(BF), n_col), "col")
        return jnp.sum(tiles.astype(F32), axis=0)

    def on_turn(turn, step, old, *operands):
        return lax.cond(turn, step, lambda old, *rest: old, old, *operands)

    known = run.astype(BF)
    for j in range(last - 1):
        arrived = lax.ppermute(known, "row", [(j, j + 1)])

        def forward(run, arrived, factor, j=j):
            return run - reduce_columns(dot_nn(arrived, factor[: (j + 1) * width]))

        run = on_turn(row_at == j + 1, forward, run, arrived, factor)
        known = jnp.concatenate([arrived, run.astype(BF)], axis=1)
        if j == last - 4:
            held, _ = lax.optimization_barrier((factor, known))
            first = jnp.where(row_at == last, 0, row_at // 2)
            at = jnp.stack([first, row_at]).astype(jnp.int32)
            folded = chunked(fold_kernel, at, whole, section, 0, (held,), 2 * width)

    def merge_pair(at, whole, folded):
        odd_part = lax.ppermute(folded, "row", down[:-1])

        def pass_through(odd_part, _=None):
            return chunked(through_kernel, at, whole, half, 2, (odd_part,), 2 * width)

        through = lax.cond(even, pass_through, lambda _, own: pass_through(own), odd_part, folded)
        low_half = lax.ppermute(through, "row", down[:-1])

        def merge_even(at, whole, through, low_half, folded):
            lefts = (through, low_half, folded)
            return chunked(merge_kernel, at, whole, section, 0, lefts, 2 * width)

        return lax.cond(
            even,
            merge_even,
            lambda at, whole, through, low_half, folded: folded,
            at,
            whole,
            through,
            low_half,
            folded,
        )

    held, _ = lax.optimization_barrier((whole, known))
    merged = lax.cond(
        row_at < last - 1,
        merge_pair,
        lambda at, whole, folded: jnp.zeros_like(folded),
        at,
        held,
        folded,
    )
    arrived = lax.ppermute(known, "row", [(last - 1, last)])
    arrived, merged = lax.optimization_barrier((arrived, merged))

    def solve_last(run, arrived, folded):
        return reduce_columns(
            dot_nn(jnp.concatenate([-arrived, run.astype(BF)], axis=1), folded)
        )

    run = on_turn(row_at == last, solve_last, run, arrived, folded)
    arrived = lax.ppermute(run.astype(BF), "row", [(last, last - 1)])

    def solve_next(run, arrived, folded):
        return reduce_columns(
            dot_nn(
                jnp.concatenate([run.astype(BF), -arrived], axis=1), folded[(last - 1) * width :]
            )
        )

    run = on_turn(row_at == last - 1, solve_next, run, arrived, folded)
    low = run.astype(BF)

    other = lax.ppermute(low, "row", down)
    zero = jnp.zeros_like(low)
    held = jnp.where(even, jnp.concatenate([low, -other], 1), jnp.concatenate([zero, low], 1))
    known = jnp.concatenate([low, arrived], axis=1)
    known = (
        lax.ppermute(known, "row", [(last - 1, last - 3)])
        + lax.ppermute(known, "row", [(last - 1, last - 2)])
    )

    def partial_sum(held, known, merged, pair):
        return dot_nn(jnp.concatenate([held, -known], axis=1), merged[2 * pair * width :])

    for pair in (2, 1):

        def backward(run, held, known, merged, pair=pair):
            return reduce_columns(partial_sum(held, known, merged, pair))

        run = on_turn(row_at // 2 == pair, backward, run, held, known, merged)
        low = run.astype(BF)
        same = [(2 * pair, 2 * pair - 2), (2 * pair + 1, 2 * pair - 1)]
        cross = [(2 * pair, 2 * pair - 1), (2 * pair + 1, 2 * pair - 2)]
        same = lax.ppermute(jnp.concatenate([low, known], axis=1), "row", same)
        cross = lax.ppermute(low, "row", cross)
        same, older = same[:, :width], same[:, width:]
        known = jnp.concatenate(
            [jnp.where(even, same, cross), jnp.where(even, cross, same), older], axis=1
        )

    def gather_rhs(low, held, known, merged):
        done = exchange(low.reshape(n_col, rhs_here, width), "col")
        return jnp.transpose(done, (1, 0, 2)).reshape(rhs_here, section).astype(F32)

    def finish(low, held, known, merged):
        partial = partial_sum(held, known, merged, 0)
        tiles = exchange(partial.astype(BF).reshape(n_col, rhs_here, section), "col")
        return jnp.sum(tiles.astype(F32), axis=0)

    root_solution = lax.cond(row_at < 2, finish, gather_rhs, low, held, known, merged)

    take = (block_rows[:, None] == root_rows.reshape(-1)[None, :]).astype(BF)
    taken = dot_nn(root_solution.astype(BF), take).astype(BF)
    taken = exchange(split_columns(taken, n_row), "row")
    taken = jnp.sum(taken.astype(F32), axis=0)
    taken = jnp.where(live[None, :], taken, 0.0).astype(BF)
    leaf_solution = solved - dot_nn(taken, interpolation[0])
    return (leaf_solution[None], root_solution)


def solution(mesh):
    in_specs = (
        P("row", "col", None),
        P("row", None, None),
        P("row", None, None),
        P("row"),
        P("row", None),
        P(),
        P("col", "row"),
        P("row", None, "col"),
    )
    out_specs = (P("row", "col", None), P("col", "row"))

    return jax.shard_map(
        on_device, mesh=mesh, in_specs=in_specs, out_specs=out_specs, check_vma=False
    )
```

```python
import jax
import jax.numpy as jnp
from jax import lax
from jax.experimental import pallas as pl
from jax.experimental.pallas import tpu as pltpu
from jax.sharding import PartitionSpec as P


BF = jnp.bfloat16
F32 = jnp.float32


def dot_nt(a, b):
    return lax.dot_general(a, b, (((1,), (1,)), ((), ())), preferred_element_type=F32)


def dot_nn(a, b):
    return lax.dot_general(a, b, (((1,), (0,)), ((), ())), preferred_element_type=F32)


def exchange(x, axis):
    return lax.all_to_all(x, axis, 0, 0, tiled=True)


def split_columns(x, parts):
    rows, width = x.shape
    return jnp.transpose(x.reshape(rows, parts, width // parts), (1, 0, 2))


def fold_kernel(at_ref, right_ref, left_ref, out_ref):
    step = pl.program_id(0)
    first, own = at_ref[0], at_ref[1]

    @pl.when(step >= first)
    def _():
        total = jnp.dot(left_ref[...], right_ref[...], preferred_element_type=F32)
        width = out_ref.shape[0] // 2
        for part in range(2):
            here = slice(part * width, (part + 1) * width)
            kept = (2 * step + part == own).astype(F32)
            out_ref[here, :] = jnp.where(
                kept > 0.5, left_ref[here, :], total[here, :].astype(out_ref.dtype)
            )


def through_kernel(at_ref, right_ref, left_ref, out_ref):
    @pl.when(pl.program_id(0) >= at_ref[0])
    def _():
        out_ref[...] = jnp.dot(
            left_ref[...], right_ref[...], preferred_element_type=F32
        ).astype(out_ref.dtype)


def merge_kernel(at_ref, right_ref, high_ref, low_ref, folded_ref, out_ref):
    step = pl.program_id(0)
    first, own = at_ref[0], at_ref[1]

    @pl.when(step >= first)
    def _():
        half = high_ref.shape[1]
        total = jnp.dot(high_ref[...], right_ref[:half, :], preferred_element_type=F32)
        total += jnp.dot(low_ref[...], right_ref[half:, :], preferred_element_type=F32)
        width = out_ref.shape[0] // 2
        for part in range(2):
            here = slice(part * width, (part + 1) * width)
            block = 2 * step + part
            kept = (block != own + 1).astype(F32)
            passed = (block != own).astype(F32)
            old = jnp.where(kept > 0.5, folded_ref[here, :].astype(F32), 0.0)
            new = jnp.where(passed > 0.5, total[here, :], 0.0)
            new = jnp.where(kept > 0.5, -new, new)
            out_ref[here, :] = (old + new).astype(out_ref.dtype)


def chunked(kernel, at, right, columns, right_block, lefts, chunk):
    def row(step, at):
        return (jnp.maximum(step, at[0]), 0)

    rows = lefts[0].shape[0]
    grid_spec = pltpu.PrefetchScalarGridSpec(
        num_scalar_prefetch=1,
        grid=(rows // chunk,),
        in_specs=[pl.BlockSpec((right.shape[0], columns), lambda step, at: (0, right_block))]
        + [pl.BlockSpec((chunk, x.shape[1]), row) for x in lefts],
        out_specs=pl.BlockSpec((chunk, columns), row),
    )
    return pl.pallas_call(
        kernel,
        grid_spec=grid_spec,
        out_shape=jax.ShapeDtypeStruct((rows, columns), BF),
    )(at, right, *lefts)


def on_device(
    leaf_rhs, leaf_inverse, interpolation, ranks, skeleton_rows, root_rows, root_rhs, root_factor
):
    row_at = lax.axis_index("row")
    n_row = lax.axis_size("row")
    n_col = lax.axis_size("col")
    rhs_here = leaf_rhs.shape[1]
    n_rhs = rhs_here * n_col
    slots = skeleton_rows.shape[1]
    section = root_rhs.shape[1]
    half = section // 2
    width = section // n_col
    leaf = leaf_rhs.shape[2]
    even = row_at % 2 == 0
    up = [(r, r + 1) for r in range(0, n_row, 2)]
    down = [(r + 1, r) for r in range(0, n_row, 2)]

    solved = dot_nt(leaf_rhs[0], leaf_inverse[0])
    live = jnp.arange(slots, dtype=jnp.int32) < ranks[0]
    chosen = jnp.where(live, skeleton_rows[0], -1)
    pick = (jnp.arange(leaf, dtype=jnp.int32)[:, None] == chosen[None, :]).astype(BF)
    skeleton = dot_nn(solved.astype(BF), pick).astype(BF)

    factor = jnp.transpose(root_factor, (1, 2, 0)).reshape(n_row * width, section)

    diagonal = lax.dynamic_slice_in_dim(factor, row_at * width, width, 0)
    above = lax.dynamic_slice_in_dim(factor, (row_at | 1) * width, width, 0)
    lower = lax.ppermute(above[:, half:], "row", up)
    held = jnp.concatenate([diagonal, jnp.where(even, above[:, :half], lower)], axis=1)
    whole = lax.all_gather(held, "col", axis=0, tiled=True)

    spread = exchange(jnp.broadcast_to(skeleton[None], (n_row, rhs_here, slots)), "row")
    spread = jnp.transpose(spread, (1, 0, 2)).reshape(rhs_here, n_row * slots)
    block_rows = row_at * section + jnp.arange(section, dtype=jnp.int32)
    place = (root_rows.reshape(-1)[:, None] == block_rows[None, :]).astype(BF)
    run = split_columns(root_rhs + dot_nn(spread, place), n_col)
    run = exchange(run, "col")
    run = run.reshape(n_rhs, width)

    last = n_row - 1

    def tiles_of(partial):
        return split_columns(partial.astype(BF), n_col)

    def take_turn(turn, run, partial, sign=0):
        def reduce_columns(run, tiles):
            total = jnp.sum(exchange(tiles, "col").astype(F32), axis=0)
            return run - total if sign else total

        return lax.cond(turn, reduce_columns, lambda run, tiles: run, run, tiles_of(partial))

    known = run.astype(BF)
    for j in range(last - 1):
        arrived = lax.ppermute(known, "row", [(j, j + 1)])
        partial = dot_nn(arrived, factor[: (j + 1) * width])
        run = take_turn(row_at == j + 1, run, partial, -1)
        known = jnp.concatenate([arrived, run.astype(BF)], axis=1)
        if j == last - 4:
            held, _ = lax.optimization_barrier((factor, known))
            first = jnp.where(row_at == last, 0, row_at // 2)
            at = jnp.stack([first, row_at]).astype(jnp.int32)
            folded = chunked(fold_kernel, at, whole, section, 0, (held,), 2 * width)

    def merge_pair(at, whole, folded):
        odd_part = lax.ppermute(folded, "row", down[:-1])

        def pass_through(odd_part, _=None):
            return chunked(through_kernel, at, whole, half, 2, (odd_part,), 2 * width)

        through = lax.cond(even, pass_through, lambda _, own: pass_through(own), odd_part, folded)
        low_half = lax.ppermute(through, "row", down[:-1])

        def merge_even(at, whole, through, low_half, folded):
            lefts = (through, low_half, folded)
            return chunked(merge_kernel, at, whole, section, 0, lefts, 2 * width)

        return lax.cond(
            even,
            merge_even,
            lambda at, whole, through, low_half, folded: folded,
            at,
            whole,
            through,
            low_half,
            folded,
        )

    arrived = lax.ppermute(known, "row", [(last - 1, last)])
    low = run.astype(BF)
    other = lax.ppermute(low, "row", down[:-1])
    zero = jnp.zeros_like(low)
    held_rhs = jnp.where(even, jnp.concatenate([low, -other], 1), jnp.concatenate([zero, low], 1))
    held, _ = lax.optimization_barrier((whole, known))
    merged = lax.cond(
        row_at < last - 1,
        merge_pair,
        lambda at, whole, folded: jnp.zeros_like(folded),
        at,
        held,
        folded,
    )
    arrived, merged = lax.optimization_barrier((arrived, merged))

    partial = dot_nn(jnp.concatenate([-arrived, low], axis=1), folded)
    run = take_turn(row_at == last, run, partial)
    seventh = run.astype(BF)
    arrived = lax.ppermute(seventh, "row", [(last, last - 1)])
    early = lax.ppermute(seventh, "row", [(last, last - 2)])
    early += lax.ppermute(seventh, "row", [(last, last - 3)])
    partial = dot_nn(jnp.concatenate([low, -arrived], axis=1), folded[(last - 1) * width :])
    run = take_turn(row_at == last - 1, run, partial)
    sixth = run.astype(BF)
    arrived = lax.ppermute(sixth, "row", [(last - 1, last - 3)])
    arrived += lax.ppermute(sixth, "row", [(last - 1, last - 2)])
    known = jnp.concatenate([arrived, early], axis=1)

    def partial_sum(known, pair):
        return dot_nn(jnp.concatenate([held_rhs, -known], axis=1), merged[2 * pair * width :])

    for pair in (2, 1):
        run = take_turn(row_at // 2 == pair, run, partial_sum(known, pair))
        low = run.astype(BF)
        same = [(2 * pair, 2 * pair - 2), (2 * pair + 1, 2 * pair - 1)]
        cross = [(2 * pair, 2 * pair - 1), (2 * pair + 1, 2 * pair - 2)]
        straight = lax.ppermute(low, "row", same)
        crossed = lax.ppermute(low, "row", cross)
        older = lax.ppermute(known, "row", same)
        known = jnp.concatenate(
            [jnp.where(even, straight, crossed), jnp.where(even, crossed, straight), older], axis=1
        )

    def gather_rhs(run, partial):
        done = exchange(run.astype(BF).reshape(n_col, rhs_here, width), "col")
        done = jnp.transpose(done, (1, 0, 2)).reshape(rhs_here, section).astype(F32)
        return lax.optimization_barrier(done)

    def finish(run, partial):
        tiles = exchange(partial.reshape(n_col, rhs_here, section), "col")
        return lax.optimization_barrier(jnp.sum(tiles.astype(F32), axis=0))

    root_solution = lax.cond(
        row_at < 2, finish, gather_rhs, run, partial_sum(known, 0).astype(BF)
    )

    take = (block_rows[:, None] == root_rows.reshape(-1)[None, :]).astype(BF)
    taken = dot_nn(root_solution.astype(BF), take).astype(BF)
    taken = exchange(split_columns(taken, n_row), "row")
    taken = jnp.sum(taken.astype(F32), axis=0)
    taken = jnp.where(live[None, :], taken, 0.0).astype(BF)
    leaf_solution = solved - dot_nn(taken, interpolation[0])
    return (leaf_solution[None], root_solution)


def solution(mesh):
    in_specs = (
        P("row", "col", None),
        P("row", None, None),
        P("row", None, None),
        P("row"),
        P("row", None),
        P(),
        P("col", "row"),
        P("row", None, "col"),
    )
    out_specs = (P("row", "col", None), P("col", "row"))

    return jax.shard_map(
        on_device, mesh=mesh, in_specs=in_specs, out_specs=out_specs, check_vma=False
    )
```

```python
import functools

import jax
import jax.numpy as jnp
from jax import lax
from jax.experimental import pallas as pl
from jax.experimental.pallas import tpu as pltpu
from jax.sharding import PartitionSpec as P


BF = jnp.bfloat16
F32 = jnp.float32


def dot_nt(a, b):
    return lax.dot_general(a, b, (((1,), (1,)), ((), ())), preferred_element_type=F32)


def dot_nn(a, b):
    return lax.dot_general(a, b, (((1,), (0,)), ((), ())), preferred_element_type=F32)


def exchange(x, axis):
    return lax.all_to_all(x, axis, 0, 0, tiled=True)


def split_columns(x, parts):
    rows, width = x.shape
    return jnp.transpose(x.reshape(rows, parts, width // parts), (1, 0, 2))


def fold_kernel(at_ref, right_ref, left_ref, out_ref):
    step = pl.program_id(0)
    first, own = at_ref[0], at_ref[1]

    @pl.when(step >= first)
    def _():
        total = jnp.dot(left_ref[...], right_ref[...], preferred_element_type=F32)
        width = out_ref.shape[0] // 2
        for part in range(2):
            here = slice(part * width, (part + 1) * width)
            kept = (2 * step + part == own).astype(F32)
            out_ref[here, :] = jnp.where(
                kept > 0.5, left_ref[here, :], total[here, :].astype(out_ref.dtype)
            )


def through_kernel(at_ref, right_ref, left_ref, out_ref):
    @pl.when(pl.program_id(0) >= at_ref[0])
    def _():
        out_ref[...] = jnp.dot(
            left_ref[...], right_ref[...], preferred_element_type=F32
        ).astype(out_ref.dtype)


def merge_kernel(at_ref, right_ref, high_ref, low_ref, folded_ref, out_ref):
    step = pl.program_id(0)
    first, own = at_ref[0], at_ref[1]

    @pl.when(step >= first)
    def _():
        half = high_ref.shape[1]
        total = jnp.dot(high_ref[...], right_ref[:half, :], preferred_element_type=F32)
        total += jnp.dot(low_ref[...], right_ref[half:, :], preferred_element_type=F32)
        width = out_ref.shape[0] // 2
        for part in range(2):
            here = slice(part * width, (part + 1) * width)
            block = 2 * step + part
            kept = (block != own + 1).astype(F32)
            passed = (block != own).astype(F32)
            old = jnp.where(kept > 0.5, folded_ref[here, :].astype(F32), 0.0)
            new = jnp.where(passed > 0.5, total[here, :], 0.0)
            new = jnp.where(kept > 0.5, -new, new)
            out_ref[here, :] = (old + new).astype(out_ref.dtype)


def chunked(kernel, at, right, columns, right_block, lefts, chunk):
    def row(step, at):
        return (jnp.maximum(step, at[0]), 0)

    rows = lefts[0].shape[0]
    grid_spec = pltpu.PrefetchScalarGridSpec(
        num_scalar_prefetch=1,
        grid=(rows // chunk,),
        in_specs=[pl.BlockSpec((right.shape[0], columns), lambda step, at: (0, right_block))]
        + [pl.BlockSpec((chunk, x.shape[1]), row) for x in lefts],
        out_specs=pl.BlockSpec((chunk, columns), row),
    )
    return pl.pallas_call(
        kernel,
        grid_spec=grid_spec,
        out_shape=jax.ShapeDtypeStruct((rows, columns), BF),
    )(at, right, *lefts)


def late_kernel(sign, x_ref, weight_ref, sums_ref, out_ref):
    total = jnp.dot(x_ref[...], weight_ref[...], preferred_element_type=F32)
    total = sums_ref[...] + total if sign > 0 else sums_ref[...] - total
    width = out_ref.shape[2]
    for tile in range(out_ref.shape[0]):
        out_ref[tile] = total[:, tile * width : (tile + 1) * width].astype(out_ref.dtype)


def late_part(x, weights, block, sums, width, sign, chunks=2):
    rows, depth = x.shape
    columns = weights.shape[1] // chunks
    tiles = weights.shape[1] // width
    return pl.pallas_call(
        functools.partial(late_kernel, sign),
        grid=(chunks,),
        in_specs=[
            pl.BlockSpec((rows, depth), lambda step: (0, 0)),
            pl.BlockSpec((depth, columns), lambda step: (block, step)),
            pl.BlockSpec((rows, columns), lambda step: (0, step)),
        ],
        out_specs=pl.BlockSpec((tiles // chunks, rows, width), lambda step: (step, 0, 0)),
        out_shape=jax.ShapeDtypeStruct((tiles, rows, width), BF),
    )(x, weights, sums)


def on_device(
    leaf_rhs, leaf_inverse, interpolation, ranks, skeleton_rows, root_rows, root_rhs, root_factor
):
    row_at = lax.axis_index("row")
    n_row = lax.axis_size("row")
    n_col = lax.axis_size("col")
    rhs_here = leaf_rhs.shape[1]
    n_rhs = rhs_here * n_col
    slots = skeleton_rows.shape[1]
    section = root_rhs.shape[1]
    half = section // 2
    width = section // n_col
    leaf = leaf_rhs.shape[2]
    even = row_at % 2 == 0
    up = [(r, r + 1) for r in range(0, n_row, 2)]
    down = [(r + 1, r) for r in range(0, n_row, 2)]

    solved = dot_nt(leaf_rhs[0], leaf_inverse[0])
    live = jnp.arange(slots, dtype=jnp.int32) < ranks[0]
    chosen = jnp.where(live, skeleton_rows[0], -1)
    pick = (jnp.arange(leaf, dtype=jnp.int32)[:, None] == chosen[None, :]).astype(BF)
    skeleton = dot_nn(solved.astype(BF), pick).astype(BF)

    factor = jnp.transpose(root_factor, (1, 2, 0)).reshape(n_row * width, section)

    diagonal = lax.dynamic_slice_in_dim(factor, row_at * width, width, 0)
    above = lax.dynamic_slice_in_dim(factor, (row_at | 1) * width, width, 0)
    lower = lax.ppermute(above[:, half:], "row", up)
    held = jnp.concatenate([diagonal, jnp.where(even, above[:, :half], lower)], axis=1)
    whole = lax.all_gather(held, "col", axis=0, tiled=True)

    spread = exchange(jnp.broadcast_to(skeleton[None], (n_row, rhs_here, slots)), "row")
    spread = jnp.transpose(spread, (1, 0, 2)).reshape(rhs_here, n_row * slots)
    block_rows = row_at * section + jnp.arange(section, dtype=jnp.int32)
    place = (root_rows.reshape(-1)[:, None] == block_rows[None, :]).astype(BF)
    run = split_columns(root_rhs + dot_nn(spread, place), n_col)
    run = exchange(run, "col")
    run = run.reshape(n_rhs, width)

    last = n_row - 1

    def tiles_of(partial):
        return split_columns(partial.astype(BF), n_col)

    def take_turn(turn, run, tiles, sign=0):
        def reduce_columns(run, tiles):
            total = jnp.sum(exchange(tiles, "col").astype(F32), axis=0)
            return run - total if sign else total

        return lax.cond(turn, reduce_columns, lambda run, tiles: run, run, tiles)

    def early_part(turn, part, *operands):
        return lax.cond(
            turn, part, lambda *rest: jnp.zeros((n_rhs, section), F32), *operands
        )

    def blocks(weights, first, count):
        return weights[first * width : (first + count) * width]

    low = run.astype(BF)
    before, sums = None, None
    for j in range(last - 1):
        arrived = lax.ppermute(low, "row", [(j, j + 1)])
        known = low if before is None else jnp.concatenate([before, low], axis=1)
        known = lax.ppermute(known, "row", [(j, j + 2)])
        late, early = sums, None
        if j < last - 2:
            early = early_part(
                row_at == j + 2, lambda x, w, j=j: dot_nn(x, blocks(w, 0, j + 1)), known, factor
            )
            arrived, early = lax.optimization_barrier((arrived, early))
        if late is None:
            tiles = tiles_of(dot_nn(arrived, blocks(factor, j, 1)))
        else:
            tiles = late_part(arrived, factor, j, late, width, 1)
        run = take_turn(row_at == j + 1, run, tiles, -1)
        low = run.astype(BF)
        before = arrived if j == 0 else jnp.concatenate([older, arrived], axis=1)
        older, sums = known, early
        if j == last - 4:
            held, _ = lax.optimization_barrier((factor, low))
            first = jnp.where(row_at == last, 0, row_at // 2)
            at = jnp.stack([first, row_at]).astype(jnp.int32)
            folded = chunked(fold_kernel, at, whole, section, 0, (held,), 2 * width)

    def merge_pair(at, whole, folded):
        odd_part = lax.ppermute(folded, "row", down[:-1])

        def pass_through(odd_part, _=None):
            return chunked(through_kernel, at, whole, half, 2, (odd_part,), 2 * width)

        through = lax.cond(even, pass_through, lambda _, own: pass_through(own), odd_part, folded)
        low_half = lax.ppermute(through, "row", down[:-1])

        def merge_even(at, whole, through, low_half, folded):
            lefts = (through, low_half, folded)
            return chunked(merge_kernel, at, whole, section, 0, lefts, 2 * width)

        return lax.cond(
            even,
            merge_even,
            lambda at, whole, through, low_half, folded: folded,
            at,
            whole,
            through,
            low_half,
            folded,
        )

    arrived = lax.ppermute(low, "row", [(last - 1, last)])
    other = lax.ppermute(low, "row", down[:-1])
    zero = jnp.zeros_like(low)
    held_rhs = jnp.where(even, jnp.concatenate([low, -other], 1), jnp.concatenate([zero, low], 1))
    held, _ = lax.optimization_barrier((whole, low))
    merged = lax.cond(
        row_at < last - 1,
        merge_pair,
        lambda at, whole, folded: jnp.zeros_like(folded),
        at,
        held,
        folded,
    )
    sums = early_part(
        row_at == last,
        lambda low, known, w: dot_nn(low, blocks(w, last, 1)) - dot_nn(known, blocks(w, 0, last - 1)),
        low,
        known,
        folded,
    )
    later = early_part(
        row_at == last - 1, lambda low, w: dot_nn(low, blocks(w, last - 1, 1)), low, folded
    )
    arrived, merged, sums, later = lax.optimization_barrier((arrived, merged, sums, later))
    run = take_turn(row_at == last, run, late_part(arrived, folded, last - 1, sums, width, -1))
    final = run.astype(BF)
    seventh = lax.ppermute(final, "row", [(last, last - 1)])
    final, seventh = lax.optimization_barrier((final, seventh))
    ahead = lax.ppermute(final, "row", [(last, last - 2)])
    ahead += lax.ppermute(final, "row", [(last, last - 3)])
    run = take_turn(row_at == last - 1, run, late_part(seventh, folded, last, later, width, -1))
    sixth = run.astype(BF)
    sums = early_part(
        row_at // 2 == 2,
        lambda held, x, w: dot_nn(held, blocks(w, 4, 2)) - dot_nn(x, blocks(w, 7, 1)),
        held_rhs,
        ahead,
        merged,
    )
    arrived = lax.ppermute(sixth, "row", [(last - 1, last - 3)])
    arrived += lax.ppermute(sixth, "row", [(last - 1, last - 2)])
    arrived, sums = lax.optimization_barrier((arrived, sums))

    run = take_turn(row_at // 2 == 2, run, late_part(arrived, merged, 6, sums, width, -1))

    sixth, _ = lax.optimization_barrier((sixth, arrived))
    both = jnp.where(
        even,
        jnp.concatenate([sixth, seventh], axis=1),
        jnp.concatenate([lax.ppermute(sixth, "row", [(last - 1, last)]), final], axis=1),
    )
    far = lax.ppermute(both, "row", [(6, 2), (7, 3)])
    farther = lax.ppermute(both, "row", [(6, 0), (7, 1)])

    def pair_sums(pair, held, x, w):
        return dot_nn(held, blocks(w, 2 * pair, 2)) - dot_nn(x, w[(2 * pair + 4) * width :])

    def next_pair(low, pair):
        straight = lax.ppermute(low, "row", [(2 * pair, 2 * pair - 2), (2 * pair + 1, 2 * pair - 1)])
        crossed = lax.ppermute(low, "row", [(2 * pair, 2 * pair - 1), (2 * pair + 1, 2 * pair - 2)])
        return jnp.concatenate(
            [jnp.where(even, straight, crossed), jnp.where(even, crossed, straight)], axis=1
        )

    sums = early_part(
        row_at // 2 == 1, lambda *rest: pair_sums(1, *rest), held_rhs, far, merged
    )
    low = run.astype(BF)
    arrived = next_pair(low, 2)
    arrived, sums = lax.optimization_barrier((arrived, sums))
    low, _ = lax.optimization_barrier((low, arrived))
    swapped = lax.ppermute(low, "row", [(4, 5), (5, 4)])
    both = jnp.where(
        even, jnp.concatenate([low, swapped], axis=1), jnp.concatenate([swapped, low], axis=1)
    )
    both = lax.ppermute(both, "row", [(4, 0), (5, 1)])
    run = take_turn(row_at // 2 == 1, run, late_part(arrived, merged, 2, sums, width, -1))
    sums = early_part(
        row_at < 2,
        lambda *rest: pair_sums(0, *rest),
        held_rhs,
        jnp.concatenate([both, farther], axis=1),
        merged,
    )
    arrived = next_pair(run.astype(BF), 1)
    arrived, sums = lax.optimization_barrier((arrived, sums))
    partial = sums - dot_nn(arrived, blocks(merged, 2, 2))

    def gather_rhs(run, partial):
        done = exchange(run.astype(BF).reshape(n_col, rhs_here, width), "col")
        done = jnp.transpose(done, (1, 0, 2)).reshape(rhs_here, section).astype(F32)
        return lax.optimization_barrier(done)

    def finish(run, partial):
        tiles = exchange(partial.reshape(n_col, rhs_here, section), "col")
        return lax.optimization_barrier(jnp.sum(tiles.astype(F32), axis=0))

    root_solution = lax.cond(
        row_at < 2, finish, gather_rhs, run, partial.astype(BF)
    )

    take = (block_rows[:, None] == root_rows.reshape(-1)[None, :]).astype(BF)
    taken = dot_nn(root_solution.astype(BF), take).astype(BF)
    taken = exchange(split_columns(taken, n_row), "row")
    taken = jnp.sum(taken.astype(F32), axis=0)
    taken = jnp.where(live[None, :], taken, 0.0).astype(BF)
    leaf_solution = solved - dot_nn(taken, interpolation[0])
    return (leaf_solution[None], root_solution)


def solution(mesh):
    in_specs = (
        P("row", "col", None),
        P("row", None, None),
        P("row", None, None),
        P("row"),
        P("row", None),
        P(),
        P("col", "row"),
        P("row", None, "col"),
    )
    out_specs = (P("row", "col", None), P("col", "row"))

    return jax.shard_map(
        on_device, mesh=mesh, in_specs=in_specs, out_specs=out_specs, check_vma=False
    )
```

```python
import jax
import jax.numpy as jnp
from jax import lax
from jax.experimental import pallas as pl
from jax.experimental.pallas import tpu as pltpu
from jax.sharding import PartitionSpec as P


BF = jnp.bfloat16
F32 = jnp.float32


def dot_nt(a, b):
    return lax.dot_general(a, b, (((1,), (1,)), ((), ())), preferred_element_type=F32)


def dot_nn(a, b):
    return lax.dot_general(a, b, (((1,), (0,)), ((), ())), preferred_element_type=F32)


def exchange(x, axis):
    return lax.all_to_all(x, axis, 0, 0, tiled=True)


def split_columns(x, parts):
    rows, width = x.shape
    return jnp.transpose(x.reshape(rows, parts, width // parts), (1, 0, 2))


def fold_kernel(at_ref, right_ref, left_ref, out_ref):
    step = pl.program_id(0)
    first, own = at_ref[0], at_ref[1]

    @pl.when(step >= first)
    def _():
        total = jnp.dot(left_ref[...], right_ref[...], preferred_element_type=F32)
        width = out_ref.shape[0] // 2
        for part in range(2):
            here = slice(part * width, (part + 1) * width)
            kept = (2 * step + part == own).astype(F32)
            out_ref[here, :] = jnp.where(
                kept > 0.5, left_ref[here, :], total[here, :].astype(out_ref.dtype)
            )


def through_kernel(at_ref, right_ref, left_ref, out_ref):
    @pl.when(pl.program_id(0) >= at_ref[0])
    def _():
        out_ref[...] = jnp.dot(
            left_ref[...], right_ref[...], preferred_element_type=F32
        ).astype(out_ref.dtype)


def merge_kernel(at_ref, right_ref, high_ref, low_ref, folded_ref, out_ref):
    step = pl.program_id(0)
    first, own = at_ref[0], at_ref[1]

    @pl.when(step >= first)
    def _():
        half = high_ref.shape[1]
        total = jnp.dot(high_ref[...], right_ref[:half, :], preferred_element_type=F32)
        total += jnp.dot(low_ref[...], right_ref[half:, :], preferred_element_type=F32)
        width = out_ref.shape[0] // 2
        for part in range(2):
            here = slice(part * width, (part + 1) * width)
            block = 2 * step + part
            kept = (block != own + 1).astype(F32)
            passed = (block != own).astype(F32)
            old = jnp.where(kept > 0.5, folded_ref[here, :].astype(F32), 0.0)
            new = jnp.where(passed > 0.5, total[here, :], 0.0)
            new = jnp.where(kept > 0.5, -new, new)
            out_ref[here, :] = (old + new).astype(out_ref.dtype)


def chunked(kernel, at, right, columns, right_block, lefts, chunk):
    def row(step, at):
        return (jnp.maximum(step, at[0]), 0)

    rows = lefts[0].shape[0]
    grid_spec = pltpu.PrefetchScalarGridSpec(
        num_scalar_prefetch=1,
        grid=(rows // chunk,),
        in_specs=[pl.BlockSpec((right.shape[0], columns), lambda step, at: (0, right_block))]
        + [pl.BlockSpec((chunk, x.shape[1]), row) for x in lefts],
        out_specs=pl.BlockSpec((chunk, columns), row),
    )
    return pl.pallas_call(
        kernel,
        grid_spec=grid_spec,
        out_shape=jax.ShapeDtypeStruct((rows, columns), BF),
    )(at, right, *lefts)


def on_device(
    leaf_rhs, leaf_inverse, interpolation, ranks, skeleton_rows, root_rows, root_rhs, root_factor
):
    row_at = lax.axis_index("row")
    n_row = lax.axis_size("row")
    n_col = lax.axis_size("col")
    rhs_here = leaf_rhs.shape[1]
    n_rhs = rhs_here * n_col
    slots = skeleton_rows.shape[1]
    section = root_rhs.shape[1]
    half = section // 2
    width = section // n_col
    leaf = leaf_rhs.shape[2]
    even = row_at % 2 == 0
    up = [(r, r + 1) for r in range(0, n_row, 2)]
    down = [(r + 1, r) for r in range(0, n_row, 2)]

    solved = dot_nt(leaf_rhs[0], leaf_inverse[0])
    live = jnp.arange(slots, dtype=jnp.int32) < ranks[0]
    chosen = jnp.where(live, skeleton_rows[0], -1)
    pick = (jnp.arange(leaf, dtype=jnp.int32)[:, None] == chosen[None, :]).astype(BF)
    skeleton = dot_nn(solved.astype(BF), pick).astype(BF)

    factor = jnp.transpose(root_factor, (1, 2, 0)).reshape(n_row * width, section)

    diagonal = lax.dynamic_slice_in_dim(factor, row_at * width, width, 0)
    above = lax.dynamic_slice_in_dim(factor, (row_at | 1) * width, width, 0)
    lower = lax.ppermute(above[:, half:], "row", up)
    held = jnp.concatenate([diagonal, jnp.where(even, above[:, :half], lower)], axis=1)
    whole = lax.all_gather(held, "col", axis=0, tiled=True)

    spread = exchange(jnp.broadcast_to(skeleton[None], (n_row, rhs_here, slots)), "row")
    spread = jnp.transpose(spread, (1, 0, 2)).reshape(rhs_here, n_row * slots)
    block_rows = row_at * section + jnp.arange(section, dtype=jnp.int32)
    place = (root_rows.reshape(-1)[:, None] == block_rows[None, :]).astype(BF)
    run = split_columns(root_rhs + dot_nn(spread, place), n_col)
    run = exchange(run, "col")
    run = run.reshape(n_rhs, width)

    last = n_row - 1

    def tiles_of(partial):
        return split_columns(partial.astype(BF), n_col)

    def take_turn(turn, run, partial, sign=0):
        def reduce_columns(run, tiles):
            total = jnp.sum(exchange(tiles, "col").astype(F32), axis=0)
            return run - total if sign else total

        return lax.cond(turn, reduce_columns, lambda run, tiles: run, run, tiles_of(partial))

    def take_whole_turn(turn, run, sign, *operands):
        def reduce_columns(run, x, weights):
            total = jnp.sum(exchange(tiles_of(dot_nn(x, weights)), "col").astype(F32), axis=0)
            return run - total if sign else total

        return lax.cond(turn, reduce_columns, lambda run, *rest: run, run, *operands)

    known = run.astype(BF)
    for j in range(last - 1):
        arrived = lax.ppermute(known, "row", [(j, j + 1)])
        if j < last - 2:
            partial = dot_nn(arrived, factor[: (j + 1) * width])
            run = take_turn(row_at == j + 1, run, partial, -1)
        else:
            run = take_whole_turn(row_at == j + 1, run, -1, arrived, factor[: (j + 1) * width])
        known = jnp.concatenate([arrived, run.astype(BF)], axis=1)
        if j == last - 4:
            held, _ = lax.optimization_barrier((factor, known))
            first = jnp.where(row_at == last, 0, row_at // 2)
            at = jnp.stack([first, row_at]).astype(jnp.int32)
            folded = chunked(fold_kernel, at, whole, section, 0, (held,), 2 * width)

    def merge_pair(at, whole, folded):
        odd_part = lax.ppermute(folded, "row", down[:-1])

        def pass_through(odd_part, _=None):
            return chunked(through_kernel, at, whole, half, 2, (odd_part,), 2 * width)

        through = lax.cond(even, pass_through, lambda _, own: pass_through(own), odd_part, folded)
        low_half = lax.ppermute(through, "row", down[:-1])

        def merge_even(at, whole, through, low_half, folded):
            lefts = (through, low_half, folded)
            return chunked(merge_kernel, at, whole, section, 0, lefts, 2 * width)

        return lax.cond(
            even,
            merge_even,
            lambda at, whole, through, low_half, folded: folded,
            at,
            whole,
            through,
            low_half,
            folded,
        )

    arrived = lax.ppermute(known, "row", [(last - 1, last)])
    low = run.astype(BF)
    other = lax.ppermute(low, "row", down[:-1])
    zero = jnp.zeros_like(low)
    held_rhs = jnp.where(even, jnp.concatenate([low, -other], 1), jnp.concatenate([zero, low], 1))
    held, _ = lax.optimization_barrier((whole, known))
    merged = lax.cond(
        row_at < last - 1,
        merge_pair,
        lambda at, whole, folded: jnp.zeros_like(folded),
        at,
        held,
        folded,
    )
    arrived, merged = lax.optimization_barrier((arrived, merged))

    run = take_whole_turn(
        row_at == last, run, 0, jnp.concatenate([-arrived, low], axis=1), folded
    )
    seventh = run.astype(BF)
    arrived = lax.ppermute(seventh, "row", [(last, last - 1)])
    early = lax.ppermute(seventh, "row", [(last, last - 2)])
    early += lax.ppermute(seventh, "row", [(last, last - 3)])
    run = take_whole_turn(
        row_at == last - 1,
        run,
        0,
        jnp.concatenate([low, -arrived], axis=1),
        folded[(last - 1) * width :],
    )
    sixth = run.astype(BF)
    newest = lax.ppermute(sixth, "row", [(last - 1, last - 3)])
    newest += lax.ppermute(sixth, "row", [(last - 1, last - 2)])
    known = jnp.concatenate([newest, early], axis=1)

    swapped = lax.ppermute(sixth, "row", [(last - 1, last)])
    both = jnp.where(
        even,
        jnp.concatenate([sixth, arrived], axis=1),
        jnp.concatenate([swapped, seventh], axis=1),
    )
    far = lax.ppermute(both, "row", [(6, 2), (7, 3)])
    farther = lax.ppermute(both, "row", [(6, 0), (7, 1)])

    def partial_sum(known, pair):
        return dot_nn(jnp.concatenate([held_rhs, -known], axis=1), merged[2 * pair * width :])

    for pair in (2, 1):
        run = take_turn(row_at // 2 == pair, run, partial_sum(known, pair))
        low = run.astype(BF)
        same = [(2 * pair, 2 * pair - 2), (2 * pair + 1, 2 * pair - 1)]
        cross = [(2 * pair, 2 * pair - 1), (2 * pair + 1, 2 * pair - 2)]
        straight = lax.ppermute(low, "row", same)
        crossed = lax.ppermute(low, "row", cross)
        newest = [jnp.where(even, straight, crossed), jnp.where(even, crossed, straight)]
        known = jnp.concatenate(newest + [far], axis=1)
        if pair == 2:
            swapped = lax.ppermute(low, "row", [(4, 5), (5, 4)])
            both = jnp.where(
                even,
                jnp.concatenate([low, swapped], axis=1),
                jnp.concatenate([swapped, low], axis=1),
            )
            both = lax.ppermute(both, "row", [(4, 0), (5, 1)])
            far = jnp.concatenate([both, farther], axis=1)

    def gather_rhs(run, partial):
        done = exchange(run.astype(BF).reshape(n_col, rhs_here, width), "col")
        done = jnp.transpose(done, (1, 0, 2)).reshape(rhs_here, section).astype(F32)
        return lax.optimization_barrier(done)

    def finish(run, partial):
        tiles = exchange(partial.reshape(n_col, rhs_here, section), "col")
        return lax.optimization_barrier(jnp.sum(tiles.astype(F32), axis=0))

    root_solution = lax.cond(
        row_at < 2, finish, gather_rhs, run, partial_sum(known, 0).astype(BF)
    )

    take = (block_rows[:, None] == root_rows.reshape(-1)[None, :]).astype(BF)
    taken = dot_nn(root_solution.astype(BF), take).astype(BF)
    taken = exchange(split_columns(taken, n_row), "row")
    taken = jnp.sum(taken.astype(F32), axis=0)
    taken = jnp.where(live[None, :], taken, 0.0).astype(BF)
    leaf_solution = solved - dot_nn(taken, interpolation[0])
    return (leaf_solution[None], root_solution)


def solution(mesh):
    in_specs = (
        P("row", "col", None),
        P("row", None, None),
        P("row", None, None),
        P("row"),
        P("row", None),
        P(),
        P("col", "row"),
        P("row", None, "col"),
    )
    out_specs = (P("row", "col", None), P("col", "row"))

    return jax.shard_map(
        on_device, mesh=mesh, in_specs=in_specs, out_specs=out_specs, check_vma=False
    )
```

```python
import jax
import jax.numpy as jnp
from jax import lax
from jax.experimental import pallas as pl
from jax.experimental.pallas import tpu as pltpu
from jax.sharding import PartitionSpec as P


BF = jnp.bfloat16
F32 = jnp.float32


def dot_nt(a, b):
    return lax.dot_general(a, b, (((1,), (1,)), ((), ())), preferred_element_type=F32)


def dot_nn(a, b):
    return lax.dot_general(a, b, (((1,), (0,)), ((), ())), preferred_element_type=F32)


def exchange(x, axis):
    return lax.all_to_all(x, axis, 0, 0, tiled=True)


def split_columns(x, parts):
    rows, width = x.shape
    return jnp.transpose(x.reshape(rows, parts, width // parts), (1, 0, 2))


def fold_kernel(at_ref, right_ref, left_ref, passed_low_ref, passed_high_ref, out_ref):
    step = pl.program_id(0)
    first, own, last = at_ref[0], at_ref[1], at_ref[2]

    @pl.when((step >= first) & (own == last) & (step < pl.num_programs(0) - 1))
    def _():
        half = passed_low_ref.shape[1]
        low = left_ref[:, :half].astype(F32) - passed_low_ref[...].astype(F32)
        high = left_ref[:, half:].astype(F32) - passed_high_ref[...].astype(F32)
        total = jnp.dot(low.astype(BF), right_ref[:half, :], preferred_element_type=F32)
        total += jnp.dot(high.astype(BF), right_ref[half:, :], preferred_element_type=F32)
        out_ref[...] = total.astype(out_ref.dtype)

    @pl.when((step >= first) & ((own != last) | (step == pl.num_programs(0) - 1)))
    def _():
        total = jnp.dot(left_ref[...], right_ref[...], preferred_element_type=F32)
        width = out_ref.shape[0] // 2
        for part in range(2):
            here = slice(part * width, (part + 1) * width)
            kept = (2 * step + part == own).astype(F32)
            out_ref[here, :] = jnp.where(
                kept > 0.5, left_ref[here, :], total[here, :].astype(out_ref.dtype)
            )


def through_kernel(at_ref, right_ref, left_ref, out_ref):
    @pl.when(pl.program_id(0) >= at_ref[0])
    def _():
        out_ref[...] = jnp.dot(
            left_ref[...], right_ref[...], preferred_element_type=F32
        ).astype(out_ref.dtype)


def merge_kernel(at_ref, right_ref, high_ref, low_ref, folded_ref, out_ref):
    step = pl.program_id(0)
    first, own = at_ref[0], at_ref[1]

    @pl.when(step >= first)
    def _():
        half = high_ref.shape[1]
        total = jnp.dot(high_ref[...], right_ref[:half, :], preferred_element_type=F32)
        total += jnp.dot(low_ref[...], right_ref[half:, :], preferred_element_type=F32)
        width = out_ref.shape[0] // 2
        for part in range(2):
            here = slice(part * width, (part + 1) * width)
            block = 2 * step + part
            kept = (block != own + 1).astype(F32)
            passed = (block != own).astype(F32)
            old = jnp.where(kept > 0.5, folded_ref[here, :].astype(F32), 0.0)
            new = jnp.where(passed > 0.5, total[here, :], 0.0)
            new = jnp.where(kept > 0.5, -new, new)
            out_ref[here, :] = (old + new).astype(out_ref.dtype)


def chunked(kernel, at, right, columns, right_block, lefts, chunk, rows=None):
    rows = lefts[0].shape[0] if rows is None else rows

    def row_map(count):
        return lambda step, at: (jnp.minimum(jnp.maximum(step, at[0]), count - 1), 0)

    grid_spec = pltpu.PrefetchScalarGridSpec(
        num_scalar_prefetch=1,
        grid=(rows // chunk,),
        in_specs=[pl.BlockSpec((right.shape[0], columns), lambda step, at: (0, right_block))]
        + [pl.BlockSpec((chunk, x.shape[1]), row_map(x.shape[0] // chunk)) for x in lefts],
        out_specs=pl.BlockSpec((chunk, columns), row_map(rows // chunk)),
    )
    return pl.pallas_call(
        kernel,
        grid_spec=grid_spec,
        out_shape=jax.ShapeDtypeStruct((rows, columns), BF),
    )(at, right, *lefts)


def on_device(
    leaf_rhs, leaf_inverse, interpolation, ranks, skeleton_rows, root_rows, root_rhs, root_factor
):
    row_at = lax.axis_index("row")
    n_row = lax.axis_size("row")
    n_col = lax.axis_size("col")
    rhs_here = leaf_rhs.shape[1]
    n_rhs = rhs_here * n_col
    slots = skeleton_rows.shape[1]
    section = root_rhs.shape[1]
    half = section // 2
    width = section // n_col
    leaf = leaf_rhs.shape[2]
    even = row_at % 2 == 0
    up = [(r, r + 1) for r in range(0, n_row, 2)]
    down = [(r + 1, r) for r in range(0, n_row, 2)]

    solved = dot_nt(leaf_rhs[0], leaf_inverse[0])
    live = jnp.arange(slots, dtype=jnp.int32) < ranks[0]
    chosen = jnp.where(live, skeleton_rows[0], -1)
    pick = (jnp.arange(leaf, dtype=jnp.int32)[:, None] == chosen[None, :]).astype(BF)
    skeleton = dot_nn(solved.astype(BF), pick).astype(BF)

    factor = jnp.transpose(root_factor, (1, 2, 0)).reshape(n_row * width, section)

    diagonal = lax.dynamic_slice_in_dim(factor, row_at * width, width, 0)
    pick_block = jnp.where(row_at == n_row - 1, n_row - 2, row_at | 1)
    above = lax.dynamic_slice_in_dim(factor, pick_block * width, width, 0)
    kept = jnp.where(even, above[:, :half], above[:, half:])
    sent = jnp.where(even, above[:, half:], above[:, :half])
    sent = lax.ppermute(sent, "row", up[:-1] + down[-1:])
    giver = (row_at < n_row - 2) == even
    held = jnp.concatenate([diagonal, jnp.where(giver, kept, sent)], axis=1)
    whole = lax.all_gather(held, "col", axis=0, tiled=True)

    spread = exchange(jnp.broadcast_to(skeleton[None], (n_row, rhs_here, slots)), "row")
    spread = jnp.transpose(spread, (1, 0, 2)).reshape(rhs_here, n_row * slots)
    block_rows = row_at * section + jnp.arange(section, dtype=jnp.int32)
    place = (root_rows.reshape(-1)[:, None] == block_rows[None, :]).astype(BF)
    run = split_columns(root_rhs + dot_nn(spread, place), n_col)
    run = exchange(run, "col")
    run = run.reshape(n_rhs, width)

    last = n_row - 1

    def tiles_of(partial):
        return split_columns(partial.astype(BF), n_col)

    def take_turn(turn, run, partial, sign=0):
        def reduce_columns(run, tiles):
            total = jnp.sum(exchange(tiles, "col").astype(F32), axis=0)
            return run - total if sign else total

        return lax.cond(turn, reduce_columns, lambda run, tiles: run, run, tiles_of(partial))

    def take_whole_turn(turn, run, sign, *operands):
        def reduce_columns(run, x, weights):
            total = jnp.sum(exchange(tiles_of(dot_nn(x, weights)), "col").astype(F32), axis=0)
            return run - total if sign else total

        return lax.cond(turn, reduce_columns, lambda run, *rest: run, run, *operands)

    low = run.astype(BF)
    known = low
    for j in range(last - 2):
        arrived = lax.ppermute(known, "row", [(j, j + 1)])
        if j == last - 3:
            ahead = lax.ppermute(known, "row", [(j, j + 2)])
        partial = dot_nn(arrived, factor[: (j + 1) * width])
        run = take_turn(row_at == j + 1, run, partial, -1)
        low = run.astype(BF)
        known = jnp.concatenate([arrived, low], axis=1)
        if j == 1:
            partner = lax.ppermute(factor, "row", [(last - 1, last)])
            partner_low = lax.ppermute(low, "row", [(last - 1, last)])
    newest = lax.ppermute(low, "row", [(last - 2, last - 1)])
    newest_last = lax.ppermute(low, "row", [(last - 2, last)])
    ahead_last = lax.ppermute(ahead, "row", [(last - 1, last)])

    def pass_on(whole, factor, partner):
        def product(left):
            return chunked(
                through_kernel,
                jnp.zeros((3,), jnp.int32),
                whole,
                half,
                2,
                (left,),
                2 * width,
                (last - 1) * width,
            )

        mine = lax.cond(even, lambda a, b: product(a), lambda a, b: product(b), factor, partner)
        return lax.ppermute(mine, "row", [(last - 1, last)]), mine

    def pass_nothing(whole, factor, partner):
        nothing = jnp.zeros(((last - 1) * width, half), BF)
        return nothing, nothing

    passed_low, passed_high = lax.cond(
        row_at >= last - 1, pass_on, pass_nothing, whole, factor, partner
    )
    known = jnp.concatenate([ahead, newest], axis=1)
    forward = low
    run = take_whole_turn(
        row_at == last - 1, run, -1, known, factor[: (last - 1) * width]
    )

    first = jnp.where(row_at == last, 0, row_at // 2)
    at = jnp.stack([first, row_at, jnp.full_like(row_at, last)]).astype(jnp.int32)
    folded = chunked(
        fold_kernel, at, whole, section, 0, (factor, passed_low, passed_high), 2 * width
    )

    def merge_pair(at, whole, folded):
        odd_part = lax.ppermute(folded, "row", down[:-1])

        def pass_through(odd_part, _=None):
            return chunked(through_kernel, at, whole, half, 2, (odd_part,), 2 * width)

        through = lax.cond(even, pass_through, lambda _, own: pass_through(own), odd_part, folded)
        low_half = lax.ppermute(through, "row", down[:-1])

        def merge_even(at, whole, through, low_half, folded):
            lefts = (through, low_half, folded)
            return chunked(merge_kernel, at, whole, section, 0, lefts, 2 * width)

        return lax.cond(
            even,
            merge_even,
            lambda at, whole, through, low_half, folded: folded,
            at,
            whole,
            through,
            low_half,
            folded,
        )

    other = lax.ppermute(forward, "row", down[:-1])
    zero = jnp.zeros_like(forward)
    held_rhs = jnp.where(
        even,
        jnp.concatenate([forward, -other], axis=1),
        jnp.concatenate([zero, forward], axis=1),
    )
    merged = lax.cond(
        row_at < last - 1, merge_pair, lambda at, whole, folded: folded, at, whole, folded
    )

    x = jnp.concatenate([-ahead_last, -newest_last, -partner_low, forward], axis=1)
    run = take_whole_turn(row_at == last, run, 0, x, merged)
    low = run.astype(BF)
    seventh = low
    arrived = lax.ppermute(seventh, "row", [(last, last - 1)])
    early = lax.ppermute(seventh, "row", [(last, last - 2)])
    early += lax.ppermute(seventh, "row", [(last, last - 3)])
    run = take_whole_turn(
        row_at == last - 1,
        run,
        0,
        jnp.concatenate([low, -arrived], axis=1),
        merged[(last - 1) * width :],
    )
    sixth = run.astype(BF)
    newest = lax.ppermute(sixth, "row", [(last - 1, last - 3)])
    newest += lax.ppermute(sixth, "row", [(last - 1, last - 2)])
    known = jnp.concatenate([newest, early], axis=1)

    swapped = lax.ppermute(sixth, "row", [(last - 1, last)])
    both = jnp.where(
        even,
        jnp.concatenate([sixth, arrived], axis=1),
        jnp.concatenate([swapped, seventh], axis=1),
    )
    far = lax.ppermute(both, "row", [(6, 2), (7, 3)])
    farther = lax.ppermute(both, "row", [(6, 0), (7, 1)])

    def partial_sum(known, pair):
        return dot_nn(jnp.concatenate([held_rhs, -known], axis=1), merged[2 * pair * width :])

    for pair in (2, 1):
        run = take_turn(row_at // 2 == pair, run, partial_sum(known, pair))
        low = run.astype(BF)
        same = [(2 * pair, 2 * pair - 2), (2 * pair + 1, 2 * pair - 1)]
        cross = [(2 * pair, 2 * pair - 1), (2 * pair + 1, 2 * pair - 2)]
        straight = lax.ppermute(low, "row", same)
        crossed = lax.ppermute(low, "row", cross)
        newest = [jnp.where(even, straight, crossed), jnp.where(even, crossed, straight)]
        known = jnp.concatenate(newest + [far], axis=1)
        if pair == 2:
            swapped = lax.ppermute(low, "row", [(4, 5), (5, 4)])
            both = jnp.where(
                even,
                jnp.concatenate([low, swapped], axis=1),
                jnp.concatenate([swapped, low], axis=1),
            )
            both = lax.ppermute(both, "row", [(4, 0), (5, 1)])
            far = jnp.concatenate([both, farther], axis=1)

    def gather_rhs(run, partial):
        done = exchange(run.astype(BF).reshape(n_col, rhs_here, width), "col")
        done = jnp.transpose(done, (1, 0, 2)).reshape(rhs_here, section).astype(F32)
        return lax.optimization_barrier(done)

    def finish(run, partial):
        tiles = exchange(partial.reshape(n_col, rhs_here, section), "col")
        return lax.optimization_barrier(jnp.sum(tiles.astype(F32), axis=0))

    root_solution = lax.cond(
        row_at < 2, finish, gather_rhs, run, partial_sum(known, 0).astype(BF)
    )

    take = (block_rows[:, None] == root_rows.reshape(-1)[None, :]).astype(BF)
    taken = dot_nn(root_solution.astype(BF), take).astype(BF)
    taken = exchange(split_columns(taken, n_row), "row")
    taken = jnp.sum(taken.astype(F32), axis=0)
    taken = jnp.where(live[None, :], taken, 0.0).astype(BF)
    leaf_solution = solved - dot_nn(taken, interpolation[0])
    return (leaf_solution[None], root_solution)


def solution(mesh):
    in_specs = (
        P("row", "col", None),
        P("row", None, None),
        P("row", None, None),
        P("row"),
        P("row", None),
        P(),
        P("col", "row"),
        P("row", None, "col"),
    )
    out_specs = (P("row", "col", None), P("col", "row"))

    return jax.shard_map(
        on_device, mesh=mesh, in_specs=in_specs, out_specs=out_specs, check_vma=False
    )
```

```python
import jax
import jax.numpy as jnp
from jax import lax
from jax.experimental import pallas as pl
from jax.experimental.pallas import tpu as pltpu
from jax.sharding import PartitionSpec as P


BF = jnp.bfloat16
F32 = jnp.float32


def dot_nt(a, b):
    return lax.dot_general(a, b, (((1,), (1,)), ((), ())), preferred_element_type=F32)


def dot_nn(a, b):
    return lax.dot_general(a, b, (((1,), (0,)), ((), ())), preferred_element_type=F32)


def exchange(x, axis):
    return lax.all_to_all(x, axis, 0, 0, tiled=True)


def split_columns(x, parts):
    rows, width = x.shape
    return jnp.transpose(x.reshape(rows, parts, width // parts), (1, 0, 2))


def fold_kernel(at_ref, right_ref, left_ref, passed_low_ref, passed_high_ref, out_ref):
    step = pl.program_id(0)
    first, own, last = at_ref[0], at_ref[1], at_ref[2]

    @pl.when((step >= first) & (own == last) & (step < pl.num_programs(0) - 1))
    def _():
        half = passed_low_ref.shape[1]
        low = left_ref[:, :half].astype(F32) - passed_low_ref[...].astype(F32)
        high = left_ref[:, half:].astype(F32) - passed_high_ref[...].astype(F32)
        total = jnp.dot(low.astype(BF), right_ref[:half, :], preferred_element_type=F32)
        total += jnp.dot(high.astype(BF), right_ref[half:, :], preferred_element_type=F32)
        out_ref[...] = total.astype(out_ref.dtype)

    @pl.when((step >= first) & ((own != last) | (step == pl.num_programs(0) - 1)))
    def _():
        total = jnp.dot(left_ref[...], right_ref[...], preferred_element_type=F32)
        width = out_ref.shape[0] // 2
        for part in range(2):
            here = slice(part * width, (part + 1) * width)
            kept = (2 * step + part == own).astype(F32)
            out_ref[here, :] = jnp.where(
                kept > 0.5, left_ref[here, :], total[here, :].astype(out_ref.dtype)
            )


def through_kernel(at_ref, right_ref, left_ref, out_ref):
    @pl.when(pl.program_id(0) >= at_ref[0])
    def _():
        out_ref[...] = jnp.dot(
            left_ref[...], right_ref[...], preferred_element_type=F32
        ).astype(out_ref.dtype)


def merge_kernel(at_ref, right_ref, high_ref, low_ref, folded_ref, out_ref):
    step = pl.program_id(0)
    first, own = at_ref[0], at_ref[1]

    @pl.when(step >= first)
    def _():
        half = high_ref.shape[1]
        total = jnp.dot(high_ref[...], right_ref[:half, :], preferred_element_type=F32)
        total += jnp.dot(low_ref[...], right_ref[half:, :], preferred_element_type=F32)
        width = out_ref.shape[0] // 2
        for part in range(2):
            here = slice(part * width, (part + 1) * width)
            block = 2 * step + part
            kept = (block != own + 1).astype(F32)
            passed = (block != own).astype(F32)
            old = jnp.where(kept > 0.5, folded_ref[here, :].astype(F32), 0.0)
            new = jnp.where(passed > 0.5, total[here, :], 0.0)
            new = jnp.where(kept > 0.5, -new, new)
            out_ref[here, :] = (old + new).astype(out_ref.dtype)


def chunked(kernel, at, right, columns, right_block, lefts, chunk, rows=None, aliases=None):
    rows = lefts[0].shape[0] if rows is None else rows

    def row_map(count):
        return lambda step, at: (jnp.minimum(jnp.maximum(step, at[0]), count - 1), 0)

    grid_spec = pltpu.PrefetchScalarGridSpec(
        num_scalar_prefetch=1,
        grid=(rows // chunk,),
        in_specs=[pl.BlockSpec((right.shape[0], columns), lambda step, at: (0, right_block))]
        + [pl.BlockSpec((chunk, x.shape[1]), row_map(x.shape[0] // chunk)) for x in lefts],
        out_specs=pl.BlockSpec((chunk, columns), row_map(rows // chunk)),
    )
    return pl.pallas_call(
        kernel,
        grid_spec=grid_spec,
        out_shape=jax.ShapeDtypeStruct((rows, columns), BF),
        input_output_aliases=aliases or {},
    )(at, right, *lefts)


def on_device(
    leaf_rhs, leaf_inverse, interpolation, ranks, skeleton_rows, root_rows, root_rhs, root_factor
):
    row_at = lax.axis_index("row")
    n_row = lax.axis_size("row")
    n_col = lax.axis_size("col")
    rhs_here = leaf_rhs.shape[1]
    n_rhs = rhs_here * n_col
    slots = skeleton_rows.shape[1]
    section = root_rhs.shape[1]
    half = section // 2
    width = section // n_col
    leaf = leaf_rhs.shape[2]
    even = row_at % 2 == 0
    up = [(r, r + 1) for r in range(0, n_row, 2)]
    down = [(r + 1, r) for r in range(0, n_row, 2)]

    solved = dot_nt(leaf_rhs[0], leaf_inverse[0])
    live = jnp.arange(slots, dtype=jnp.int32) < ranks[0]
    chosen = jnp.where(live, skeleton_rows[0], -1)
    pick = (jnp.arange(leaf, dtype=jnp.int32)[:, None] == chosen[None, :]).astype(BF)
    skeleton = dot_nn(solved.astype(BF), pick).astype(BF)

    factor = jnp.transpose(root_factor, (1, 2, 0)).reshape(n_row * width, section)

    diagonal = lax.dynamic_slice_in_dim(factor, row_at * width, width, 0)
    pick_block = jnp.where(row_at == n_row - 1, n_row - 2, row_at | 1)
    above = lax.dynamic_slice_in_dim(factor, pick_block * width, width, 0)
    kept = jnp.where(even, above[:, :half], above[:, half:])
    sent = jnp.where(even, above[:, half:], above[:, :half])
    sent = lax.ppermute(sent, "row", up[:-1] + down[-1:])
    giver = (row_at < n_row - 2) == even
    held = jnp.concatenate([diagonal, jnp.where(giver, kept, sent)], axis=1)
    whole = lax.all_gather(held, "col", axis=0, tiled=True)

    spread = exchange(jnp.broadcast_to(skeleton[None], (n_row, rhs_here, slots)), "row")
    spread = jnp.transpose(spread, (1, 0, 2)).reshape(rhs_here, n_row * slots)
    block_rows = row_at * section + jnp.arange(section, dtype=jnp.int32)
    place = (root_rows.reshape(-1)[:, None] == block_rows[None, :]).astype(BF)
    run = split_columns(root_rhs + dot_nn(spread, place), n_col)
    run = exchange(run, "col")
    run = run.reshape(n_rhs, width)

    last = n_row - 1

    def tiles_of(partial):
        return split_columns(partial.astype(BF), n_col)

    def take_turn(turn, run, partial, sign=0):
        def reduce_columns(run, tiles):
            total = jnp.sum(exchange(tiles, "col").astype(F32), axis=0)
            return run - total if sign else total

        return lax.cond(turn, reduce_columns, lambda run, tiles: run, run, tiles_of(partial))

    def take_whole_turn(turn, run, sign, *operands):
        def reduce_columns(run, x, weights):
            total = jnp.sum(exchange(tiles_of(dot_nn(x, weights)), "col").astype(F32), axis=0)
            return run - total if sign else total

        return lax.cond(turn, reduce_columns, lambda run, *rest: run, run, *operands)

    low = run.astype(BF)
    known = low
    for j in range(last - 2):
        arrived = lax.ppermute(known, "row", [(j, j + 1)])
        if j == last - 3:
            ahead = lax.ppermute(known, "row", [(j, j + 2)])
        partial = dot_nn(arrived, factor[: (j + 1) * width])
        run = take_turn(row_at == j + 1, run, partial, -1)
        low = run.astype(BF)
        known = jnp.concatenate([arrived, low], axis=1)
        if j == 1:
            partner = lax.ppermute(factor, "row", [(last - 1, last)])
            partner_low = lax.ppermute(low, "row", [(last - 1, last)])
    newest = lax.ppermute(low, "row", [(last - 2, last - 1)])
    newest_last = lax.ppermute(low, "row", [(last - 2, last)])
    ahead_last = lax.ppermute(ahead, "row", [(last - 1, last)])

    def pass_on(whole, factor, partner):
        def product(left):
            return chunked(
                through_kernel,
                jnp.zeros((3,), jnp.int32),
                whole,
                half,
                2,
                (left,),
                2 * width,
                (last - 1) * width,
            )

        mine = lax.cond(even, lambda a, b: product(a), lambda a, b: product(b), factor, partner)
        return lax.ppermute(mine, "row", [(last - 1, last)]), mine

    def pass_nothing(whole, factor, partner):
        nothing = jnp.zeros(((last - 1) * width, half), BF)
        return nothing, nothing

    passed_low, passed_high = lax.cond(
        row_at >= last - 1, pass_on, pass_nothing, whole, factor, partner
    )
    known = jnp.concatenate([ahead, newest], axis=1)
    forward = low
    run = take_whole_turn(
        row_at == last - 1, run, -1, known, factor[: (last - 1) * width]
    )

    first = jnp.where(row_at == last, 0, row_at // 2)
    at = jnp.stack([first, row_at, jnp.full_like(row_at, last)]).astype(jnp.int32)
    folded = chunked(
        fold_kernel, at, whole, section, 0, (factor, passed_low, passed_high), 2 * width
    )

    def merge_pair(at, whole, folded):
        odd_part = lax.ppermute(folded, "row", down[:-1])

        def pass_through(odd_part, _=None):
            return chunked(through_kernel, at, whole, half, 2, (odd_part,), 2 * width)

        through = lax.cond(even, pass_through, lambda _, own: pass_through(own), odd_part, folded)
        low_half = lax.ppermute(through, "row", down[:-1])

        def merge_even(at, whole, through, low_half, folded):
            lefts = (through, low_half, folded)
            aliases = {4: 0}
            return chunked(
                merge_kernel, at, whole, section, 0, lefts, 2 * width, aliases=aliases
            )

        return lax.cond(
            even,
            merge_even,
            lambda at, whole, through, low_half, folded: folded,
            at,
            whole,
            through,
            low_half,
            folded,
        )

    other = lax.ppermute(forward, "row", down[:-1])
    zero = jnp.zeros_like(forward)
    held_rhs = jnp.where(
        even,
        jnp.concatenate([forward, -other], axis=1),
        jnp.concatenate([zero, forward], axis=1),
    )
    merged = lax.cond(
        row_at < last - 1, merge_pair, lambda at, whole, folded: folded, at, whole, folded
    )

    x = jnp.concatenate([-ahead_last, -newest_last, -partner_low, forward], axis=1)
    run = take_whole_turn(row_at == last, run, 0, x, merged)
    low = run.astype(BF)
    seventh = low
    arrived = lax.ppermute(seventh, "row", [(last, last - 1)])
    early = lax.ppermute(seventh, "row", [(last, last - 2)])
    early += lax.ppermute(seventh, "row", [(last, last - 3)])
    run = take_whole_turn(
        row_at == last - 1,
        run,
        0,
        jnp.concatenate([low, -arrived], axis=1),
        merged[(last - 1) * width :],
    )
    sixth = run.astype(BF)
    newest = lax.ppermute(sixth, "row", [(last - 1, last - 3)])
    newest += lax.ppermute(sixth, "row", [(last - 1, last - 2)])
    known = jnp.concatenate([newest, early], axis=1)

    swapped = lax.ppermute(sixth, "row", [(last - 1, last)])
    both = jnp.where(
        even,
        jnp.concatenate([sixth, arrived], axis=1),
        jnp.concatenate([swapped, seventh], axis=1),
    )
    far = lax.ppermute(both, "row", [(6, 2), (7, 3)])
    farther = lax.ppermute(both, "row", [(6, 0), (7, 1)])

    def partial_sum(known, pair):
        return dot_nn(jnp.concatenate([held_rhs, -known], axis=1), merged[2 * pair * width :])

    for pair in (2, 1):
        run = take_turn(row_at // 2 == pair, run, partial_sum(known, pair))
        low = run.astype(BF)
        same = [(2 * pair, 2 * pair - 2), (2 * pair + 1, 2 * pair - 1)]
        cross = [(2 * pair, 2 * pair - 1), (2 * pair + 1, 2 * pair - 2)]
        straight = lax.ppermute(low, "row", same)
        crossed = lax.ppermute(low, "row", cross)
        newest = [jnp.where(even, straight, crossed), jnp.where(even, crossed, straight)]
        known = jnp.concatenate(newest + [far], axis=1)
        if pair == 2:
            swapped = lax.ppermute(low, "row", [(4, 5), (5, 4)])
            both = jnp.where(
                even,
                jnp.concatenate([low, swapped], axis=1),
                jnp.concatenate([swapped, low], axis=1),
            )
            both = lax.ppermute(both, "row", [(4, 0), (5, 1)])
            far = jnp.concatenate([both, farther], axis=1)

    def gather_rhs(run, partial):
        done = exchange(run.astype(BF).reshape(n_col, rhs_here, width), "col")
        done = jnp.transpose(done, (1, 0, 2)).reshape(rhs_here, section).astype(F32)
        return lax.optimization_barrier(done)

    def finish(run, partial):
        tiles = exchange(partial.reshape(n_col, rhs_here, section), "col")
        return lax.optimization_barrier(jnp.sum(tiles.astype(F32), axis=0))

    root_solution = lax.cond(
        row_at < 2, finish, gather_rhs, run, partial_sum(known, 0).astype(BF)
    )

    take = (block_rows[:, None] == root_rows.reshape(-1)[None, :]).astype(BF)
    taken = dot_nn(root_solution.astype(BF), take).astype(BF)
    taken = exchange(split_columns(taken, n_row), "row")
    taken = jnp.sum(taken.astype(F32), axis=0)
    taken = jnp.where(live[None, :], taken, 0.0).astype(BF)
    leaf_solution = solved - dot_nn(taken, interpolation[0])
    return (leaf_solution[None], root_solution)


def solution(mesh):
    in_specs = (
        P("row", "col", None),
        P("row", None, None),
        P("row", None, None),
        P("row"),
        P("row", None),
        P(),
        P("col", "row"),
        P("row", None, "col"),
    )
    out_specs = (P("row", "col", None), P("col", "row"))

    return jax.shard_map(
        on_device, mesh=mesh, in_specs=in_specs, out_specs=out_specs, check_vma=False
    )
```

```python
import jax
import jax.numpy as jnp
from jax import lax
from jax.experimental import pallas as pl
from jax.experimental.pallas import tpu as pltpu
from jax.sharding import PartitionSpec as P


BF = jnp.bfloat16
F32 = jnp.float32


def dot_nt(a, b):
    return lax.dot_general(a, b, (((1,), (1,)), ((), ())), preferred_element_type=F32)


def dot_nn(a, b):
    return lax.dot_general(a, b, (((1,), (0,)), ((), ())), preferred_element_type=F32)


def exchange(x, axis):
    return lax.all_to_all(x, axis, 0, 0, tiled=True)


def split_columns(x, parts):
    rows, width = x.shape
    return jnp.transpose(x.reshape(rows, parts, width // parts), (1, 0, 2))


def fold_kernel(at_ref, right_ref, left_ref, passed_low_ref, passed_high_ref, out_ref):
    part_of, step = pl.program_id(0), pl.program_id(1)
    first, own, last = at_ref[0], at_ref[1], at_ref[2]
    final = pl.num_programs(1) - 1
    columns = out_ref.shape[1]

    @pl.when((step >= first) & (own == last) & (step < final))
    def _():
        half = passed_low_ref.shape[1]
        low = left_ref[:, :half].astype(F32) - passed_low_ref[...].astype(F32)
        high = left_ref[:, half:].astype(F32) - passed_high_ref[...].astype(F32)
        total = jnp.dot(low.astype(BF), right_ref[:half, :], preferred_element_type=F32)
        total += jnp.dot(high.astype(BF), right_ref[half:, :], preferred_element_type=F32)
        out_ref[...] = total.astype(out_ref.dtype)

    @pl.when((step >= first) & ((own != last) | (step == final)))
    def _():
        total = jnp.dot(left_ref[...], right_ref[...], preferred_element_type=F32)
        width = out_ref.shape[0] // 2
        for part in range(2):
            here = slice(part * width, (part + 1) * width)
            kept = (2 * step + part == own).astype(F32)
            old = left_ref[here, pl.ds(pl.multiple_of(part_of * columns, columns), columns)]
            out_ref[here, :] = jnp.where(kept > 0.5, old, total[here, :].astype(out_ref.dtype))


def through_kernel(at_ref, right_ref, left_ref, out_ref):
    @pl.when(pl.program_id(1) >= at_ref[0])
    def _():
        out_ref[...] = jnp.dot(
            left_ref[...], right_ref[...], preferred_element_type=F32
        ).astype(out_ref.dtype)


def merge_kernel(at_ref, right_ref, high_ref, low_ref, folded_ref, out_ref):
    step = pl.program_id(1)
    first, own = at_ref[0], at_ref[1]

    @pl.when(step >= first)
    def _():
        half = high_ref.shape[1]
        total = jnp.dot(high_ref[...], right_ref[:half, :], preferred_element_type=F32)
        total += jnp.dot(low_ref[...], right_ref[half:, :], preferred_element_type=F32)
        width = out_ref.shape[0] // 2
        for part in range(2):
            here = slice(part * width, (part + 1) * width)
            block = 2 * step + part
            kept = (block != own + 1).astype(F32)
            passed = (block != own).astype(F32)
            old = jnp.where(kept > 0.5, folded_ref[here, :].astype(F32), 0.0)
            new = jnp.where(passed > 0.5, total[here, :], 0.0)
            new = jnp.where(kept > 0.5, -new, new)
            out_ref[here, :] = (old + new).astype(out_ref.dtype)


def chunked(kernel, at, right, columns, right_block, lefts, chunk, rows=None, aliases=None):
    rows = lefts[0].shape[0] if rows is None else rows
    part = columns // 2

    def left_spec(index, x):
        count = x.shape[0] // chunk

        def whole(side, step, at):
            return (jnp.minimum(jnp.maximum(step, at[0]), count - 1), 0)

        def halves(side, step, at):
            return (jnp.minimum(jnp.maximum(step, at[0]), count - 1), side)

        if aliases and index + 2 in aliases:
            return pl.BlockSpec((chunk, part), halves)
        return pl.BlockSpec((chunk, x.shape[1]), whole)

    def out_map(side, step, at):
        return (jnp.minimum(jnp.maximum(step, at[0]), rows // chunk - 1), side)

    grid_spec = pltpu.PrefetchScalarGridSpec(
        num_scalar_prefetch=1,
        grid=(2, rows // chunk),
        in_specs=[
            pl.BlockSpec(
                (right.shape[0], part), lambda side, step, at: (0, 2 * right_block + side)
            )
        ]
        + [left_spec(index, x) for index, x in enumerate(lefts)],
        out_specs=pl.BlockSpec((chunk, part), out_map),
    )
    return pl.pallas_call(
        kernel,
        grid_spec=grid_spec,
        out_shape=jax.ShapeDtypeStruct((rows, columns), BF),
        input_output_aliases=aliases or {},
    )(at, right, *lefts)


def on_device(
    leaf_rhs, leaf_inverse, interpolation, ranks, skeleton_rows, root_rows, root_rhs, root_factor
):
    row_at = lax.axis_index("row")
    n_row = lax.axis_size("row")
    n_col = lax.axis_size("col")
    rhs_here = leaf_rhs.shape[1]
    n_rhs = rhs_here * n_col
    slots = skeleton_rows.shape[1]
    section = root_rhs.shape[1]
    half = section // 2
    width = section // n_col
    leaf = leaf_rhs.shape[2]
    even = row_at % 2 == 0
    up = [(r, r + 1) for r in range(0, n_row, 2)]
    down = [(r + 1, r) for r in range(0, n_row, 2)]

    solved = dot_nt(leaf_rhs[0], leaf_inverse[0])
    live = jnp.arange(slots, dtype=jnp.int32) < ranks[0]
    chosen = jnp.where(live, skeleton_rows[0], -1)
    pick = (jnp.arange(leaf, dtype=jnp.int32)[:, None] == chosen[None, :]).astype(BF)
    skeleton = dot_nn(solved.astype(BF), pick).astype(BF)

    factor = jnp.transpose(root_factor, (1, 2, 0)).reshape(n_row * width, section)

    diagonal = lax.dynamic_slice_in_dim(factor, row_at * width, width, 0)
    pick_block = jnp.where(row_at == n_row - 1, n_row - 2, row_at | 1)
    above = lax.dynamic_slice_in_dim(factor, pick_block * width, width, 0)
    kept = jnp.where(even, above[:, :half], above[:, half:])
    sent = jnp.where(even, above[:, half:], above[:, :half])
    sent = lax.ppermute(sent, "row", up[:-1] + down[-1:])
    giver = (row_at < n_row - 2) == even
    held = jnp.concatenate([diagonal, jnp.where(giver, kept, sent)], axis=1)
    whole = lax.all_gather(held, "col", axis=0, tiled=True)

    spread = exchange(jnp.broadcast_to(skeleton[None], (n_row, rhs_here, slots)), "row")
    spread = jnp.transpose(spread, (1, 0, 2)).reshape(rhs_here, n_row * slots)
    block_rows = row_at * section + jnp.arange(section, dtype=jnp.int32)
    place = (root_rows.reshape(-1)[:, None] == block_rows[None, :]).astype(BF)
    run = split_columns(root_rhs + dot_nn(spread, place), n_col)
    run = exchange(run, "col")
    run = run.reshape(n_rhs, width)

    last = n_row - 1

    def tiles_of(partial):
        return split_columns(partial.astype(BF), n_col)

    def take_turn(turn, run, partial, sign=0):
        def reduce_columns(run, tiles):
            total = jnp.sum(exchange(tiles, "col").astype(F32), axis=0)
            return run - total if sign else total

        return lax.cond(turn, reduce_columns, lambda run, tiles: run, run, tiles_of(partial))

    def reduce_product(x, weights):
        return jnp.sum(exchange(tiles_of(dot_nn(x, weights)), "col").astype(F32), axis=0)

    def take_whole_turn(turn, run, *operands):
        return lax.cond(
            turn,
            lambda run, x, weights: reduce_product(x, weights),
            lambda run, *rest: run,
            run,
            *operands,
        )

    low = run.astype(BF)
    known = low
    for j in range(last - 2):
        arrived = lax.ppermute(known, "row", [(j, j + 1)])
        if j == last - 3:
            ahead = lax.ppermute(known, "row", [(j, j + 2)])
        partial = dot_nn(arrived, factor[: (j + 1) * width])
        run = take_turn(row_at == j + 1, run, partial, -1)
        low = run.astype(BF)
        known = jnp.concatenate([arrived, low], axis=1)
        if j == 1:
            partner = lax.ppermute(factor, "row", [(last - 1, last)])
            partner_low = lax.ppermute(low, "row", [(last - 1, last)])
    newest = lax.ppermute(low, "row", [(last - 2, last - 1)])
    newest_last = lax.ppermute(low, "row", [(last - 2, last)])
    ahead_last = lax.ppermute(ahead, "row", [(last - 1, last)])

    def pass_on(whole, factor, partner):
        def product(left):
            return chunked(
                through_kernel,
                jnp.zeros((3,), jnp.int32),
                whole,
                half,
                2,
                (left,),
                2 * width,
                (last - 1) * width,
            )

        mine = lax.cond(even, lambda a, b: product(a), lambda a, b: product(b), factor, partner)
        return lax.ppermute(mine, "row", [(last - 1, last)]), mine

    def pass_nothing(whole, factor, partner):
        shape = jax.ShapeDtypeStruct(((last - 1) * width, half), BF)
        anywhere = pl.BlockSpec(memory_space=pl.ANY)
        return pl.pallas_call(
            lambda low_ref, high_ref: None,
            out_shape=(shape, shape),
            out_specs=(anywhere, anywhere),
        )()

    passed_low, passed_high = lax.cond(
        row_at >= last - 1, pass_on, pass_nothing, whole, factor, partner
    )
    forward = low
    run = lax.cond(
        row_at == last - 1,
        lambda run, ahead, newest, factor: run
        - reduce_product(jnp.concatenate([ahead, newest], axis=1), factor[: (last - 1) * width]),
        lambda run, *rest: run,
        run,
        ahead,
        newest,
        factor,
    )

    first = jnp.where(row_at == last, 0, row_at // 2)
    at = jnp.stack([first, row_at, jnp.full_like(row_at, last)]).astype(jnp.int32)
    folded = chunked(
        fold_kernel, at, whole, section, 0, (factor, passed_low, passed_high), 2 * width
    )

    def merge_pair(at, whole, folded):
        odd_part = lax.ppermute(folded, "row", down[:-1])

        def pass_through(odd_part, _=None):
            return chunked(through_kernel, at, whole, half, 2, (odd_part,), 2 * width)

        through = lax.cond(even, pass_through, lambda _, own: pass_through(own), odd_part, folded)
        low_half = lax.ppermute(through, "row", down[:-1])

        def merge_even(at, whole, through, low_half, folded):
            lefts = (through, low_half, folded)
            aliases = {4: 0}
            return chunked(
                merge_kernel, at, whole, section, 0, lefts, 2 * width, aliases=aliases
            )

        return lax.cond(
            even,
            merge_even,
            lambda at, whole, through, low_half, folded: folded,
            at,
            whole,
            through,
            low_half,
            folded,
        )

    other = lax.ppermute(forward, "row", down[:-1])
    zero = jnp.zeros_like(forward)
    held_rhs = jnp.where(
        even,
        jnp.concatenate([forward, -other], axis=1),
        jnp.concatenate([zero, forward], axis=1),
    )
    merged = lax.cond(
        row_at < last - 1, merge_pair, lambda at, whole, folded: folded, at, whole, folded
    )

    x = jnp.concatenate([-ahead_last, -newest_last, -partner_low, forward], axis=1)
    run = take_whole_turn(row_at == last, run, x, merged)
    low = run.astype(BF)
    seventh = low
    arrived = lax.ppermute(seventh, "row", [(last, last - 1)])
    early = lax.ppermute(seventh, "row", [(last, last - 2)])
    early += lax.ppermute(seventh, "row", [(last, last - 3)])
    run = take_whole_turn(
        row_at == last - 1,
        run,
        jnp.concatenate([low, -arrived], axis=1),
        merged[(last - 1) * width :],
    )
    sixth = run.astype(BF)
    newest = lax.ppermute(sixth, "row", [(last - 1, last - 3)])
    newest += lax.ppermute(sixth, "row", [(last - 1, last - 2)])
    known = jnp.concatenate([newest, early], axis=1)

    swapped = lax.ppermute(sixth, "row", [(last - 1, last)])
    both = jnp.where(
        even,
        jnp.concatenate([sixth, arrived], axis=1),
        jnp.concatenate([swapped, seventh], axis=1),
    )
    far = lax.ppermute(both, "row", [(6, 2), (7, 3)])
    farther = lax.ppermute(both, "row", [(6, 0), (7, 1)])

    def partial_sum(known, pair):
        return dot_nn(jnp.concatenate([held_rhs, -known], axis=1), merged[2 * pair * width :])

    for pair in (2, 1):
        run = take_turn(row_at // 2 == pair, run, partial_sum(known, pair))
        low = run.astype(BF)
        same = [(2 * pair, 2 * pair - 2), (2 * pair + 1, 2 * pair - 1)]
        cross = [(2 * pair, 2 * pair - 1), (2 * pair + 1, 2 * pair - 2)]
        straight = lax.ppermute(low, "row", same)
        crossed = lax.ppermute(low, "row", cross)
        newest = [jnp.where(even, straight, crossed), jnp.where(even, crossed, straight)]
        known = jnp.concatenate(newest + [far], axis=1)
        if pair == 2:
            swapped = lax.ppermute(low, "row", [(4, 5), (5, 4)])
            both = jnp.where(
                even,
                jnp.concatenate([low, swapped], axis=1),
                jnp.concatenate([swapped, low], axis=1),
            )
            both = lax.ppermute(both, "row", [(4, 0), (5, 1)])
            far = jnp.concatenate([both, farther], axis=1)

    def gather_rhs(run, partial):
        done = exchange(run.astype(BF).reshape(n_col, rhs_here, width), "col")
        done = jnp.transpose(done, (1, 0, 2)).reshape(rhs_here, section).astype(F32)
        return lax.optimization_barrier(done)

    def finish(run, partial):
        tiles = exchange(partial.reshape(n_col, rhs_here, section), "col")
        return lax.optimization_barrier(jnp.sum(tiles.astype(F32), axis=0))

    root_solution = lax.cond(
        row_at < 2, finish, gather_rhs, run, partial_sum(known, 0).astype(BF)
    )

    take = (block_rows[:, None] == root_rows.reshape(-1)[None, :]).astype(BF)
    taken = dot_nn(root_solution.astype(BF), take).astype(BF)
    taken = exchange(split_columns(taken, n_row), "row")
    taken = jnp.sum(taken.astype(F32), axis=0)
    taken = jnp.where(live[None, :], taken, 0.0).astype(BF)
    leaf_solution = solved - dot_nn(taken, interpolation[0])
    return (leaf_solution[None], root_solution)


def solution(mesh):
    in_specs = (
        P("row", "col", None),
        P("row", None, None),
        P("row", None, None),
        P("row"),
        P("row", None),
        P(),
        P("col", "row"),
        P("row", None, "col"),
    )
    out_specs = (P("row", "col", None), P("col", "row"))

    return jax.shard_map(
        on_device, mesh=mesh, in_specs=in_specs, out_specs=out_specs, check_vma=False
    )
```

```python
import jax
import jax.numpy as jnp
from jax import lax
from jax.experimental import pallas as pl
from jax.experimental.pallas import tpu as pltpu
from jax.sharding import PartitionSpec as P


BF = jnp.bfloat16
F32 = jnp.float32


def dot_nt(a, b):
    return lax.dot_general(a, b, (((1,), (1,)), ((), ())), preferred_element_type=F32)


def dot_nn(a, b):
    return lax.dot_general(a, b, (((1,), (0,)), ((), ())), preferred_element_type=F32)


def exchange(x, axis):
    return lax.all_to_all(x, axis, 0, 0, tiled=True)


def split_columns(x, parts):
    rows, width = x.shape
    return jnp.transpose(x.reshape(rows, parts, width // parts), (1, 0, 2))


def fold_kernel(at_ref, right_ref, left_ref, passed_low_ref, passed_high_ref, out_ref):
    step = pl.program_id(0)
    first, own, last = at_ref[0], at_ref[1], at_ref[2]

    @pl.when((step >= first) & (own == last) & (step < pl.num_programs(0) - 1))
    def _():
        half = passed_low_ref.shape[1]
        low = left_ref[:, :half].astype(F32) - passed_low_ref[...].astype(F32)
        high = left_ref[:, half:].astype(F32) - passed_high_ref[...].astype(F32)
        total = jnp.dot(low.astype(BF), right_ref[:half, :], preferred_element_type=F32)
        total += jnp.dot(high.astype(BF), right_ref[half:, :], preferred_element_type=F32)
        out_ref[...] = total.astype(out_ref.dtype)

    @pl.when((step >= first) & ((own != last) | (step == pl.num_programs(0) - 1)))
    def _():
        total = jnp.dot(left_ref[...], right_ref[...], preferred_element_type=F32)
        width = out_ref.shape[0] // 2
        for part in range(2):
            here = slice(part * width, (part + 1) * width)
            kept = (2 * step + part == own).astype(F32)
            out_ref[here, :] = jnp.where(
                kept > 0.5, left_ref[here, :], total[here, :].astype(out_ref.dtype)
            )


def through_kernel(at_ref, right_ref, left_ref, out_ref):
    @pl.when(pl.program_id(0) >= at_ref[0])
    def _():
        out_ref[...] = jnp.dot(
            left_ref[...], right_ref[...], preferred_element_type=F32
        ).astype(out_ref.dtype)


def merge_kernel(at_ref, right_ref, high_ref, low_ref, folded_ref, out_ref):
    step = pl.program_id(0)
    first, own = at_ref[0], at_ref[1]

    @pl.when(step >= first)
    def _():
        half = high_ref.shape[1]
        total = jnp.dot(high_ref[...], right_ref[:half, :], preferred_element_type=F32)
        total += jnp.dot(low_ref[...], right_ref[half:, :], preferred_element_type=F32)
        width = out_ref.shape[0] // 2
        for part in range(2):
            here = slice(part * width, (part + 1) * width)
            block = 2 * step + part
            kept = (block != own + 1).astype(F32)
            passed = (block != own).astype(F32)
            old = jnp.where(kept > 0.5, folded_ref[here, :].astype(F32), 0.0)
            new = jnp.where(passed > 0.5, total[here, :], 0.0)
            new = jnp.where(kept > 0.5, -new, new)
            out_ref[here, :] = (old + new).astype(out_ref.dtype)


def chunked(kernel, at, right, columns, right_block, lefts, chunk, rows=None, aliases=None):
    rows = lefts[0].shape[0] if rows is None else rows

    def row_map(count):
        return lambda step, at: (jnp.minimum(jnp.maximum(step, at[0]), count - 1), 0)

    grid_spec = pltpu.PrefetchScalarGridSpec(
        num_scalar_prefetch=1,
        grid=(rows // chunk,),
        in_specs=[pl.BlockSpec((right.shape[0], columns), lambda step, at: (0, right_block))]
        + [pl.BlockSpec((chunk, x.shape[1]), row_map(x.shape[0] // chunk)) for x in lefts],
        out_specs=pl.BlockSpec((chunk, columns), row_map(rows // chunk)),
    )
    return pl.pallas_call(
        kernel,
        grid_spec=grid_spec,
        out_shape=jax.ShapeDtypeStruct((rows, columns), BF),
        input_output_aliases=aliases or {},
    )(at, right, *lefts)


def on_device(
    leaf_rhs, leaf_inverse, interpolation, ranks, skeleton_rows, root_rows, root_rhs, root_factor
):
    row_at = lax.axis_index("row")
    n_row = lax.axis_size("row")
    n_col = lax.axis_size("col")
    rhs_here = leaf_rhs.shape[1]
    n_rhs = rhs_here * n_col
    slots = skeleton_rows.shape[1]
    section = root_rhs.shape[1]
    half = section // 2
    width = section // n_col
    leaf = leaf_rhs.shape[2]
    even = row_at % 2 == 0
    up = [(r, r + 1) for r in range(0, n_row, 2)]
    down = [(r + 1, r) for r in range(0, n_row, 2)]

    solved = dot_nt(leaf_rhs[0], leaf_inverse[0])
    live = jnp.arange(slots, dtype=jnp.int32) < ranks[0]
    chosen = jnp.where(live, skeleton_rows[0], -1)
    pick = (jnp.arange(leaf, dtype=jnp.int32)[:, None] == chosen[None, :]).astype(BF)
    skeleton = dot_nn(solved.astype(BF), pick).astype(BF)

    factor = jnp.transpose(root_factor, (1, 2, 0)).reshape(n_row * width, section)

    diagonal = lax.dynamic_slice_in_dim(factor, row_at * width, width, 0)
    pick_block = jnp.where(row_at == n_row - 1, n_row - 2, row_at | 1)
    above = lax.dynamic_slice_in_dim(factor, pick_block * width, width, 0)
    kept = jnp.where(even, above[:, :half], above[:, half:])
    sent = jnp.where(even, above[:, half:], above[:, :half])
    sent = lax.ppermute(sent, "row", up[:-1] + down[-1:])
    giver = (row_at < n_row - 2) == even
    held = jnp.concatenate([diagonal, jnp.where(giver, kept, sent)], axis=1)
    whole = lax.all_gather(held, "col", axis=0, tiled=True)

    spread = exchange(jnp.broadcast_to(skeleton[None], (n_row, rhs_here, slots)), "row")
    spread = jnp.transpose(spread, (1, 0, 2)).reshape(rhs_here, n_row * slots)
    block_rows = row_at * section + jnp.arange(section, dtype=jnp.int32)
    place = (root_rows.reshape(-1)[:, None] == block_rows[None, :]).astype(BF)
    run = split_columns(root_rhs + dot_nn(spread, place), n_col)
    run = exchange(run, "col")
    run = run.reshape(n_rhs, width)

    last = n_row - 1

    def tiles_of(partial):
        return split_columns(partial.astype(BF), n_col)

    def take_turn(turn, run, partial, sign=0):
        def reduce_columns(run, tiles):
            total = jnp.sum(exchange(tiles, "col").astype(F32), axis=0)
            return run - total if sign else total

        return lax.cond(turn, reduce_columns, lambda run, tiles: run, run, tiles_of(partial))

    def reduce_product(x, weights):
        return jnp.sum(exchange(tiles_of(dot_nn(x, weights)), "col").astype(F32), axis=0)

    def take_whole_turn(turn, run, *operands):
        return lax.cond(
            turn,
            lambda run, x, weights: reduce_product(x, weights),
            lambda run, *rest: run,
            run,
            *operands,
        )

    low = run.astype(BF)
    known = low
    for j in range(last - 2):
        arrived = lax.ppermute(known, "row", [(j, j + 1)])
        if j == last - 3:
            ahead = lax.ppermute(known, "row", [(j, j + 2)])
        partial = dot_nn(arrived, factor[: (j + 1) * width])
        run = take_turn(row_at == j + 1, run, partial, -1)
        low = run.astype(BF)
        known = jnp.concatenate([arrived, low], axis=1)
        if j == 1:
            partner = lax.ppermute(factor, "row", [(last - 1, last)])
            partner_low = lax.ppermute(low, "row", [(last - 1, last)])
    newest = lax.ppermute(low, "row", [(last - 2, last - 1)])
    newest_last = lax.ppermute(low, "row", [(last - 2, last)])
    ahead_last = lax.ppermute(ahead, "row", [(last - 1, last)])

    def pass_on(whole, factor, partner):
        def product(left):
            return chunked(
                through_kernel,
                jnp.zeros((3,), jnp.int32),
                whole,
                half,
                2,
                (left,),
                2 * width,
                (last - 1) * width,
            )

        mine = lax.cond(even, lambda a, b: product(a), lambda a, b: product(b), factor, partner)
        return lax.ppermute(mine, "row", [(last - 1, last)]), mine

    def pass_nothing(whole, factor, partner):
        shape = jax.ShapeDtypeStruct(((last - 1) * width, half), BF)
        anywhere = pl.BlockSpec(memory_space=pl.ANY)
        return pl.pallas_call(
            lambda low_ref, high_ref: None,
            out_shape=(shape, shape),
            out_specs=(anywhere, anywhere),
        )()

    passed_low, passed_high = lax.cond(
        row_at >= last - 1, pass_on, pass_nothing, whole, factor, partner
    )
    forward = low
    run = lax.cond(
        row_at == last - 1,
        lambda run, ahead, newest, factor: run
        - reduce_product(jnp.concatenate([ahead, newest], axis=1), factor[: (last - 1) * width]),
        lambda run, *rest: run,
        run,
        ahead,
        newest,
        factor,
    )

    first = jnp.where(row_at == last, 0, row_at // 2)
    at = jnp.stack([first, row_at, jnp.full_like(row_at, last)]).astype(jnp.int32)
    folded = chunked(
        fold_kernel, at, whole, section, 0, (factor, passed_low, passed_high), 2 * width
    )

    def merge_pair(at, whole, folded):
        odd_part = lax.ppermute(folded, "row", down[:-1])

        def pass_through(odd_part, _=None):
            return chunked(through_kernel, at, whole, half, 2, (odd_part,), 2 * width)

        through = lax.cond(even, pass_through, lambda _, own: pass_through(own), odd_part, folded)
        low_half = lax.ppermute(through, "row", down[:-1])

        def merge_even(at, whole, through, low_half, folded):
            lefts = (through, low_half, folded)
            aliases = {4: 0}
            return chunked(
                merge_kernel, at, whole, section, 0, lefts, 2 * width, aliases=aliases
            )

        return lax.cond(
            even,
            merge_even,
            lambda at, whole, through, low_half, folded: folded,
            at,
            whole,
            through,
            low_half,
            folded,
        )

    other = lax.ppermute(forward, "row", down[:-1])
    zero = jnp.zeros_like(forward)
    held_rhs = jnp.where(
        even,
        jnp.concatenate([forward, -other], axis=1),
        jnp.concatenate([zero, forward], axis=1),
    )
    merged = lax.cond(
        row_at < last - 1, merge_pair, lambda at, whole, folded: folded, at, whole, folded
    )

    x = jnp.concatenate([-ahead_last, -newest_last, -partner_low, forward], axis=1)
    run = take_whole_turn(row_at == last, run, x, merged)
    low = run.astype(BF)
    seventh = low
    arrived = lax.ppermute(seventh, "row", [(last, last - 1)])
    early = lax.ppermute(seventh, "row", [(last, last - 2)])
    early += lax.ppermute(seventh, "row", [(last, last - 3)])
    run = take_whole_turn(
        row_at == last - 1,
        run,
        jnp.concatenate([low, -arrived], axis=1),
        merged[(last - 1) * width :],
    )
    sixth = run.astype(BF)
    newest = lax.ppermute(sixth, "row", [(last - 1, last - 3)])
    newest += lax.ppermute(sixth, "row", [(last - 1, last - 2)])
    known = jnp.concatenate([newest, early], axis=1)

    swapped = lax.ppermute(sixth, "row", [(last - 1, last)])
    both = jnp.where(
        even,
        jnp.concatenate([sixth, arrived], axis=1),
        jnp.concatenate([swapped, seventh], axis=1),
    )
    far = lax.ppermute(both, "row", [(6, 2), (7, 3)])
    farther = lax.ppermute(both, "row", [(6, 0), (7, 1)])

    def partial_sum(known, pair):
        return dot_nn(jnp.concatenate([held_rhs, -known], axis=1), merged[2 * pair * width :])

    for pair in (2, 1):
        run = take_turn(row_at // 2 == pair, run, partial_sum(known, pair))
        low = run.astype(BF)
        same = [(2 * pair, 2 * pair - 2), (2 * pair + 1, 2 * pair - 1)]
        cross = [(2 * pair, 2 * pair - 1), (2 * pair + 1, 2 * pair - 2)]
        straight = lax.ppermute(low, "row", same)
        crossed = lax.ppermute(low, "row", cross)
        newest = [jnp.where(even, straight, crossed), jnp.where(even, crossed, straight)]
        known = jnp.concatenate(newest + [far], axis=1)
        if pair == 2:
            swapped = lax.ppermute(low, "row", [(4, 5), (5, 4)])
            both = jnp.where(
                even,
                jnp.concatenate([low, swapped], axis=1),
                jnp.concatenate([swapped, low], axis=1),
            )
            both = lax.ppermute(both, "row", [(4, 0), (5, 1)])
            far = jnp.concatenate([both, farther], axis=1)

    def gather_rhs(run, partial):
        done = exchange(run.astype(BF).reshape(n_col, rhs_here, width), "col")
        done = jnp.transpose(done, (1, 0, 2)).reshape(rhs_here, section).astype(F32)
        return lax.optimization_barrier(done)

    def finish(run, partial):
        tiles = exchange(partial.reshape(n_col, rhs_here, section), "col")
        return lax.optimization_barrier(jnp.sum(tiles.astype(F32), axis=0))

    root_solution = lax.cond(
        row_at < 2, finish, gather_rhs, run, partial_sum(known, 0).astype(BF)
    )

    take = (block_rows[:, None] == root_rows.reshape(-1)[None, :]).astype(BF)
    taken = dot_nn(root_solution.astype(BF), take).astype(BF)
    taken = exchange(split_columns(taken, n_row), "row")
    taken = jnp.sum(taken.astype(F32), axis=0)
    taken = jnp.where(live[None, :], taken, 0.0).astype(BF)
    leaf_solution = solved - dot_nn(taken, interpolation[0])
    return (leaf_solution[None], root_solution)


def solution(mesh):
    in_specs = (
        P("row", "col", None),
        P("row", None, None),
        P("row", None, None),
        P("row"),
        P("row", None),
        P(),
        P("col", "row"),
        P("row", None, "col"),
    )
    out_specs = (P("row", "col", None), P("col", "row"))

    return jax.shard_map(
        on_device, mesh=mesh, in_specs=in_specs, out_specs=out_specs, check_vma=False
    )
```
